32 devices in a mesh: pair: 8 (over z, x), occ: 4 (over y, core).
Axes of the slice: x: 2, y: 2, z: 4, core: 2. Of those that a mesh axis runs over, the one named last changes fastest.
Arguments:
- integrals: bfloat16 [8, 64, 64, 1024], P('pair', None, None, 'occ'), may hold values from -6 to 6
- occ_coeffs: bfloat16 [6144, 128], replicated, may hold values from -0.125 to 0.125
- virt_coeffs: bfloat16 [6144, 5120], P(None, 'pair'), may hold values from -0.078125 to 0.078125
- block_ids: int32 [2, 8, 64], P(None, 'pair'), may hold values from 0 to 95, as said below
- live_mask: int32 [8, 64], P('pair'), may hold values from 0 to 1, as said below
Outputs:
- factors: bfloat16 [128, 16, 5120], P('occ', None, 'pair')
The draws below stay inside these ranges and needn't reach their ends.
Inputs may be any that keep to these rules, and one draw needn't show every extreme that they name: `block_ids`: slot s of pair index p holds a nu block N with N // 12 == s // 8; each (mu block, nu block) pair is held by at most one slot of all pair indices. `live_mask`: among the 8 slots s with the same s // 8 of one pair index, at most 4 are 1, and exactly 4 for some such group of every pair index.
All inputs are finite; a program needn't handle non-finite values.
Results may differ from the reference program's by a relative error of at most 0.017.
Values may be sent and summed in bfloat16 or wider, within the bound.
No kernel may reach another device: no remote copies, remote signals or barrier semaphores. Data moves between devices by JAX's collectives and lax.ppermute only.
A program may use at most 64 MiB of HBM per device.

```python
import jax
import jax.numpy as jnp
from jax import lax

NB = 96
BS = 64
NBF = 6144
AUX = 16
OB = 128
NV = 5120
GROUP = 8
LIVE = 4
SLOTS = 64
N_PAIR = 8


def block_table(base_key):
    owned_count = NB // N_PAIR

    def per_owner(owner_index):
        ranking = jax.random.permutation(jax.random.fold_in(base_key, owner_index), owned_count * NB)
        ranking = ranking[:GROUP * N_PAIR]
        mu_part = ranking // owned_count
        nu_part = owner_index * owned_count + ranking % owned_count
        return jnp.stack([mu_part, nu_part]).reshape(2, N_PAIR, GROUP)
    table = jax.vmap(per_owner)(jnp.arange(N_PAIR))
    return jnp.transpose(table, (1, 2, 0, 3)).reshape(2, N_PAIR, N_PAIR * GROUP).astype(jnp.int32)


def draw_block_ids(key, part):
    return block_table(jax.random.fold_in(key, 11))


def draw_live_mask(key, part):
    count_key, rank_key = jax.random.split(jax.random.fold_in(key, 23))
    counts = jax.random.randint(count_key, (N_PAIR, N_PAIR), 1, LIVE + 1)
    diagonal = jnp.arange(N_PAIR)[:, None] == jnp.arange(N_PAIR)[None, :]
    counts = jnp.where(diagonal, LIVE, counts)
    scores = jax.random.randint(rank_key, (N_PAIR, N_PAIR, GROUP), 0, 1 << 20) * GROUP + jnp.arange(GROUP)
    rank_table = jnp.argsort(jnp.argsort(scores, axis=2), axis=2)
    flags = (rank_table < counts[:, :, None]).astype(jnp.int32)
    return flags.reshape(N_PAIR, N_PAIR * GROUP)


def levels(stream_key, dims, cuts, least, top_value):
    level = 1.0
    for axis_at, parts in cuts:
        heights = jax.random.uniform(jax.random.fold_in(jax.random.fold_in(stream_key, 6), axis_at), (parts,), jnp.float32, least / len(cuts), top_value / len(cuts))
        level = level * jnp.repeat(jnp.exp(heights), dims[axis_at] // parts).reshape((-1,) + (1,) * (len(dims) - 1 - axis_at))
    return level


def gaussian(own_key, extent, scale, most, cuts=(), kind=jnp.bfloat16):
    level = levels(own_key, extent, cuts, -0.22, 0.18) if cuts else 1.0
    values = jax.random.normal(own_key, extent, jnp.float32) * scale * level
    return jnp.minimum(jnp.maximum(values, -most), most).astype(kind)


def setup_inputs(seed: int = 0) -> dict:
    key_of = jax.random.split(jax.random.key(seed), 6)
    integrals = gaussian(key_of[0], (N_PAIR, SLOTS, BS, AUX * BS), 1.0, 6.0, ((0, 8), (3, 4)))
    occ_coeffs = gaussian(key_of[1], (NBF, OB), (32 * BS) ** -0.5, 0.125)
    virt_coeffs = gaussian(key_of[2], (NBF, NV), NBF ** -0.5, 0.078125, ((1, 8),))
    block_ids = draw_block_ids(jax.random.fold_in(key_of[5], 71), 0)
    live_mask = draw_live_mask(jax.random.fold_in(key_of[5], 71), 0)
    return {"integrals": integrals, "occ_coeffs": occ_coeffs, "virt_coeffs": virt_coeffs, "block_ids": block_ids, "live_mask": live_mask}


def reference(integrals, occ_coeffs, virt_coeffs, block_ids, live_mask):
    coeff_blocks = occ_coeffs.astype(jnp.float32).reshape(NB, BS, OB)

    def scan_step(running, inputs):
        block_data, mu_index, nu_index, live_flags = inputs
        coeff_rows = coeff_blocks[mu_index]
        shaped = block_data.astype(jnp.float32).reshape(SLOTS, BS, AUX, BS)
        partial_terms = jnp.einsum("snqm,smi->snqi", shaped, coeff_rows, precision=lax.Precision.HIGHEST)
        partial_terms = partial_terms * live_flags.astype(jnp.float32)[:, None, None, None]
        return running.at[nu_index].add(partial_terms), None

    start_sums = jnp.zeros((NB, BS, AUX, OB), jnp.float32)
    running, _ = lax.scan(scan_step, start_sums, (integrals, block_ids[0], block_ids[1], live_mask))
    half_sums = running.astype(jnp.bfloat16).reshape(NBF, AUX * OB)
    product = jnp.dot(half_sums.T, virt_coeffs, preferred_element_type=jnp.float32)
    return product.reshape(AUX, OB, NV).transpose(1, 0, 2).astype(jnp.bfloat16)
```

```python
import functools

import jax
import jax.numpy as jnp
from jax import lax
from jax.experimental import pallas as pl
from jax.experimental.pallas import tpu as pltpu
from jax.sharding import PartitionSpec as P

LIVE = 4
TAIL = 16


def pack_kernel(owned, ids_ref, live_ref, blocks_ref, out_ref, pick_ref, sems):
    owners = out_ref.shape[0]
    width = blocks_ref.shape[1]
    group = live_ref.shape[1] // owners
    row = lax.broadcasted_iota(jnp.int32, (TAIL, 128), 0)
    lane = lax.broadcasted_iota(jnp.int32, (TAIL, 128), 1)

    def copy(owner, k, slot):
        return pltpu.make_async_copy(
            blocks_ref.at[slot],
            out_ref.at[owner, pl.ds(k * width, width), :],
            sems.at[owner, k],
        )

    @pl.loop(0, owners)
    def _(owner):
        base = owner * group
        count = jnp.int32(0)
        for j in range(group):
            pick_ref[jnp.minimum(count, LIVE)] = base + j
            count = count + live_ref[0, base + j]
        tile = jnp.zeros((TAIL, 128), jnp.int32)
        for k in range(LIVE):
            slot = jnp.where(k < count, pick_ref[k], base)
            copy(owner, k, slot).start()
            mu = ids_ref[0, 0, slot]
            nu = jnp.where(k < count, lax.rem(ids_ref[1, 0, slot], owned), owned)
            tile = jnp.where((row == 0) & (lane == k), mu, tile)
            tile = jnp.where((row == 0) & (lane == LIVE + k), nu, tile)
        out_ref[owner, LIVE * width :, :128] = tile.astype(jnp.float32).astype(jnp.bfloat16)
        if out_ref.shape[2] > 128:
            out_ref[owner, LIVE * width :, 128:] = jnp.zeros(
                (TAIL, out_ref.shape[2] - 128), jnp.bfloat16
            )

    @pl.loop(0, owners)
    def _(owner):
        for k in range(LIVE):
            copy(owner, k, 0).wait()


def pack(block_ids, live_mask, blocks, owners, owned):
    slots, width, minor = blocks.shape
    rows = LIVE * width + TAIL
    return pl.pallas_call(
        functools.partial(pack_kernel, owned),
        out_shape=jax.ShapeDtypeStruct((owners, rows, minor), jnp.bfloat16),
        in_specs=[
            pl.BlockSpec(memory_space=pltpu.SMEM),
            pl.BlockSpec(memory_space=pltpu.SMEM),
            pl.BlockSpec(memory_space=pl.ANY),
        ],
        out_specs=pl.BlockSpec(memory_space=pltpu.VMEM),
        scratch_shapes=[
            pltpu.SMEM((LIVE + 1,), jnp.int32),
            pltpu.SemaphoreType.DMA((owners, LIVE)),
        ],
        name="pack_live",
    )(block_ids, live_mask, blocks)


def half_kernel(owned, width, me_ref, got_ref, coeff_ref, *refs):
    out_refs = refs[:-4]
    ids_vmem, ids_smem, total, sem = refs[-4:]
    owners = got_ref.shape[0]
    aux = got_ref.shape[2] // width
    for p in range(owners):
        ids_vmem[p : p + 1, :] = (
            got_ref[p, LIVE * width :, :128][0:1].astype(jnp.float32).astype(jnp.int32)
        )
    ids = pltpu.make_async_copy(ids_vmem, ids_smem, sem)
    ids.start()
    total[...] = jnp.zeros_like(total)
    ids.wait()

    @pl.loop(0, owners)
    def _(p):
        for k in range(LIVE):
            mu = ids_smem[p, k]
            nu = ids_smem[p, LIVE + k]
            block = got_ref[p, k * width : (k + 1) * width, :]
            stacked = jnp.concatenate(
                [block[:, q * width : (q + 1) * width] for q in range(aux)], axis=0
            )
            coeff = coeff_ref[pl.ds(pl.multiple_of(mu * width, width), width), :]
            total[nu] += lax.dot_general(
                coeff, stacked, (((0,), (1,)), ((), ())), preferred_element_type=jnp.float32
            )

    slab = total.shape[1] // len(out_refs)
    for j, out_ref in enumerate(out_refs):
        start = pl.multiple_of((me_ref[0] ^ j) * slab, slab)
        for b in range(0, owned, 2):
            pair = [total[c, pl.ds(start, slab), :] for c in range(b, min(b + 2, owned))]
            for q in range(aux):
                cut = [t[:, q * width : (q + 1) * width] for t in pair]
                piece = cut[0] if len(cut) == 1 else jnp.concatenate(cut, axis=1)
                out_ref[q * slab : (q + 1) * slab, b * width : b * width + piece.shape[1]] = (
                    piece.astype(jnp.bfloat16)
                )


def half_transform(me, got, coeffs, owned, width, occ):
    owners, _, minor = got.shape
    aux = minor // width
    occ_count = coeffs.shape[1]
    shape = jax.ShapeDtypeStruct((aux * occ_count // occ, owned * width), jnp.bfloat16)
    vmem = pl.BlockSpec(memory_space=pltpu.VMEM)
    return pl.pallas_call(
        functools.partial(half_kernel, owned, width),
        out_shape=[shape] * occ,
        in_specs=[pl.BlockSpec(memory_space=pltpu.SMEM), vmem, vmem],
        out_specs=[vmem] * occ,
        scratch_shapes=[
            pltpu.VMEM((owners, 128), jnp.int32),
            pltpu.SMEM((owners, 128), jnp.int32),
            pltpu.VMEM((owned + 1, occ_count, minor), jnp.float32),
            pltpu.SemaphoreType.DMA,
        ],
        name="half_transform",
    )(me, got, coeffs)


def on_device(integrals, occ_coeffs, virt_coeffs, block_ids, live_mask):
    blocks = integrals[0]
    width = blocks.shape[1]
    aux_local = blocks.shape[2] // width
    occ_count = occ_coeffs.shape[1]
    owners = lax.axis_size("pair")
    occ = lax.axis_size("occ")
    owned = occ_coeffs.shape[0] // width // owners
    slab = occ_count // occ
    me = lax.axis_index("occ").astype(jnp.int32)
    here = lax.axis_index("pair")

    send = pack(block_ids, live_mask, blocks, owners, owned)
    got = lax.all_to_all(send, "pair", split_axis=0, concat_axis=0, tiled=True)
    halves = half_transform(me.reshape(1), got, occ_coeffs, owned, width, occ)

    def across(array, j):
        if j == 0:
            return array
        return lax.ppermute(array, "occ", [(o, o ^ j) for o in range(occ)])

    outer = owners // 2

    def along(array):
        return lax.ppermute(
            array, "pair", [(p, (p // 2 + 1) % outer * 2 + p % 2) for p in range(owners)]
        )

    def swap(array):
        return lax.ppermute(array, "pair", [(p, p ^ 1) for p in range(owners)])

    rows = owned * width

    def gather_dot(piece):
        total = None

        def add(total, array, shift, flip):
            source = (here // 2 - shift) % outer * 2 + (here % 2 ^ flip)
            part = lax.dynamic_slice_in_dim(virt_coeffs, source * rows, rows, axis=0)
            term = jnp.dot(array, part, preferred_element_type=jnp.float32)
            return term if total is None else total + term

        for shift in range(outer):
            following = along(piece) if shift < outer - 1 else None
            other = swap(piece)
            total = add(total, piece, shift, 0)
            total = add(total, other, shift, 1)
            piece = following
        return total

    chunk = max(occ // 2, 1)
    results = []
    for first in range(0, occ, chunk):
        parts = [across(halves[j], j) for j in range(first, first + chunk)]
        piece = jnp.concatenate(parts, axis=0) if len(parts) > 1 else parts[0]
        results.append(gather_dot(piece).astype(jnp.bfloat16))
    result = jnp.concatenate(results, axis=0).reshape(occ, aux_local, slab, -1)
    bit = 1
    while bit < occ:
        swapped = result.reshape(occ // (2 * bit), 2, bit, aux_local, slab, -1)[:, ::-1]
        result = jnp.where(me & bit, swapped.reshape(result.shape), result)
        bit *= 2
    return result.reshape(occ * aux_local, slab, -1).transpose(1, 0, 2)


def solution(mesh):
    return jax.shard_map(
        on_device,
        mesh=mesh,
        in_specs=(
            P("pair", None, None, "occ"),
            P(),
            P(None, "pair"),
            P(None, "pair", None),
            P("pair", None),
        ),
        out_specs=P("occ", None, "pair"),
        check_vma=False,
    )
```

```python
import functools

import jax
import jax.numpy as jnp
from jax import lax
from jax.experimental import pallas as pl
from jax.experimental.pallas import tpu as pltpu
from jax.sharding import PartitionSpec as P


LIVE = 4
TAIL = 16
GRANT = 16 * 2**20


def pack_kernel(owned, ids_ref, live_ref, blocks_ref, *refs):
    out_refs = refs[:-2]
    pick_ref, sems = refs[-2:]
    owners, _, lanes = out_refs[0].shape
    width = blocks_ref.shape[1]
    group = live_ref.shape[1] // owners
    row = lax.broadcasted_iota(jnp.int32, (TAIL, 128), 0)
    lane = lax.broadcasted_iota(jnp.int32, (TAIL, 128), 1)

    def copy(owner, k, slot, c):
        return pltpu.make_async_copy(
            blocks_ref.at[slot, :, pl.ds(c * lanes, lanes)],
            out_refs[c].at[owner, pl.ds(k * width, width), :],
            sems.at[owner, k, c],
        )

    @pl.loop(0, owners)
    def _(owner):
        base = owner * group
        count = jnp.int32(0)
        for j in range(group):
            pick_ref[jnp.minimum(count, LIVE)] = base + j
            count = count + live_ref[0, base + j]
        tile = jnp.zeros((TAIL, 128), jnp.int32)
        for k in range(LIVE):
            slot = jnp.where(k < count, pick_ref[k], base)
            for c in range(len(out_refs)):
                copy(owner, k, slot, c).start()
            mu = ids_ref[0, 0, slot]
            nu = jnp.where(k < count, lax.rem(ids_ref[1, 0, slot], owned), owned)
            tile = jnp.where((row == 0) & (lane == k), mu, tile)
            tile = jnp.where((row == 0) & (lane == LIVE + k), nu, tile)
        out_refs[0][owner, LIVE * width :, :] = tile.astype(jnp.float32).astype(jnp.bfloat16)

    @pl.loop(0, owners)
    def _(owner):
        for k in range(LIVE):
            for c in range(len(out_refs)):
                copy(owner, k, 0, c).wait()


def pack(block_ids, live_mask, blocks, owners, owned):
    _, width, minor = blocks.shape
    chunks = minor // 128
    shapes = [
        jax.ShapeDtypeStruct((owners, LIVE * width + (0 if c else TAIL), 128), jnp.bfloat16)
        for c in range(chunks)
    ]
    return pl.pallas_call(
        functools.partial(pack_kernel, owned),
        out_shape=shapes,
        in_specs=[
            pl.BlockSpec(memory_space=pltpu.SMEM),
            pl.BlockSpec(memory_space=pltpu.SMEM),
            pl.BlockSpec(memory_space=pl.ANY),
        ],
        out_specs=[pl.BlockSpec(memory_space=pltpu.VMEM)] * chunks,
        scratch_shapes=[
            pltpu.SMEM((LIVE + 1,), jnp.int32),
            pltpu.SemaphoreType.DMA((owners, LIVE, chunks)),
        ],
        compiler_params=pltpu.CompilerParams(vmem_limit_bytes=GRANT),
        name="pack_live",
    )(block_ids, live_mask, blocks)


def half_kernel(owned, width, me_ref, tail_ref, got_ref, coeff_ref, *refs):
    out_refs = refs[:-4]
    ids_vmem, ids_smem, total, sem = refs[-4:]
    owners = got_ref.shape[0]
    aux = got_ref.shape[2] // width
    for p in range(owners):
        ids_vmem[p : p + 1, :] = tail_ref[p, 0:1, :].astype(jnp.float32).astype(jnp.int32)
    ids = pltpu.make_async_copy(ids_vmem, ids_smem, sem)
    ids.start()
    total[...] = jnp.zeros_like(total)
    ids.wait()

    @pl.loop(0, owners)
    def _(p):
        for k in range(LIVE):
            mu = ids_smem[p, k]
            nu = ids_smem[p, LIVE + k]
            block = got_ref[p, k * width : (k + 1) * width, :]
            stacked = jnp.concatenate(
                [block[:, q * width : (q + 1) * width] for q in range(aux)], axis=0
            )
            coeff = coeff_ref[pl.ds(pl.multiple_of(mu * width, width), width), :]
            total[nu] += lax.dot_general(
                coeff, stacked, (((0,), (1,)), ((), ())), preferred_element_type=jnp.float32
            )

    slab = total.shape[1] // len(out_refs)
    for j, out_ref in enumerate(out_refs):
        start = pl.multiple_of((me_ref[0] ^ j) * slab, slab)
        for b in range(0, owned, 2):
            pair = [total[c, pl.ds(start, slab), :] for c in range(b, min(b + 2, owned))]
            for q in range(aux):
                cut = [t[:, q * width : (q + 1) * width] for t in pair]
                piece = cut[0] if len(cut) == 1 else jnp.concatenate(cut, axis=1)
                out_ref[q * slab : (q + 1) * slab, b * width : b * width + piece.shape[1]] = (
                    piece.astype(jnp.bfloat16)
                )


def half_transform(me, first, got, coeffs, owned, width, occ):
    owners, _, lanes = got.shape
    aux = lanes // width
    occ_count = coeffs.shape[1]
    shape = jax.ShapeDtypeStruct((aux * occ_count // occ, owned * width), jnp.bfloat16)
    vmem = pl.BlockSpec(memory_space=pltpu.VMEM)

    def whole(*dims):
        return pl.BlockSpec(dims, lambda g: (0,) * len(dims))

    return pl.pallas_call(
        functools.partial(half_kernel, owned, width),
        grid=(1,),
        out_shape=[shape] * occ,
        in_specs=[
            pl.BlockSpec(memory_space=pltpu.SMEM),
            pl.BlockSpec((owners, TAIL, lanes), lambda g: (0, LIVE * width // TAIL, 0)),
            pl.BlockSpec((owners, LIVE * width, lanes), lambda g: (0, 0, 0)),
            whole(*coeffs.shape),
        ],
        out_specs=[whole(*shape.shape)] * occ,
        scratch_shapes=[
            pltpu.VMEM((owners, lanes), jnp.int32),
            pltpu.SMEM((owners, lanes), jnp.int32),
            pltpu.VMEM((owned + 1, occ_count, lanes), jnp.float32),
            pltpu.SemaphoreType.DMA,
        ],
        cost_estimate=pl.CostEstimate(
            flops=2 * owners * LIVE * width * lanes * occ_count,
            bytes_accessed=2 * (got.size + coeffs.size + occ * shape.size),
            transcendentals=0,
        ),
        compiler_params=pltpu.CompilerParams(vmem_limit_bytes=GRANT),
        name="half_transform",
    )(me, first, got, coeffs)


def place_kernel(occ, me_ref, *refs):
    in_refs, (out_ref, wide) = refs[:-2], refs[-2:]
    slab, aux, _ = out_ref.shape
    chunks = len(in_refs)
    local = aux // (occ * chunks)
    for c, in_ref in enumerate(in_refs):
        for j in range(occ):
            for q in range(local):
                at = (me_ref[0] ^ j) * (chunks * local) + c * local + q
                row = (j * local + q) * slab
                for t in range(wide.shape[0]):
                    wide[t, pl.ds(at, slab, stride=aux), :] = in_ref[
                        row : row + slab, t * 128 : (t + 1) * 128
                    ]
    for t in range(wide.shape[0]):
        out_ref[:, :, t * 128 : (t + 1) * 128] = (
            wide[t].reshape(slab, aux, 128).astype(out_ref.dtype)
        )


def place(me, parts, occ, slab):
    rows, columns = parts[0].shape
    aux = rows * len(parts) // slab
    vmem = pl.BlockSpec(memory_space=pltpu.VMEM)
    return pl.pallas_call(
        functools.partial(place_kernel, occ),
        out_shape=jax.ShapeDtypeStruct((slab, aux, columns), jnp.bfloat16),
        in_specs=[pl.BlockSpec(memory_space=pltpu.SMEM)] + [vmem] * len(parts),
        out_specs=vmem,
        scratch_shapes=[pltpu.VMEM((columns // 128, slab * aux, 128), jnp.float32)],
        compiler_params=pltpu.CompilerParams(vmem_limit_bytes=GRANT),
        name="place",
    )(me, *parts)


def on_device(integrals, occ_coeffs, virt_coeffs, block_ids, live_mask):
    blocks = integrals[0]
    width = blocks.shape[1]
    occ_count = occ_coeffs.shape[1]
    owners = lax.axis_size("pair")
    occ = lax.axis_size("occ")
    owned = occ_coeffs.shape[0] // width // owners
    slab = occ_count // occ
    outer = owners // 2
    rows = owned * width
    me = lax.axis_index("occ").astype(jnp.int32)
    here = lax.axis_index("pair")

    def across(array, j):
        if j == 0:
            return array
        return lax.ppermute(array, "occ", [(o, o ^ j) for o in range(occ)])

    def along(array):
        return lax.ppermute(
            array, "pair", [(p, (p // 2 + 1) % outer * 2 + p % 2) for p in range(owners)]
        )

    def swap(array):
        return lax.ppermute(array, "pair", [(p, p ^ 1) for p in range(owners)])

    def gather(piece, last):
        own, other = [piece], [swap(piece)]
        for shift in range(1, outer):
            own.append(along(own[-1]))
            if last and shift == outer - 1:
                other.append(along(other[-1]))
            else:
                other.append(swap(own[-1]))
        return own, other

    def second_half(own, other):
        total = None
        for shift in range(outer):
            for flip, array in enumerate((own[shift], other[shift])):
                source = (here // 2 - shift) % outer * 2 + (here % 2 ^ flip)
                part = lax.dynamic_slice_in_dim(virt_coeffs, source * rows, rows, axis=0)
                term = jnp.dot(array, part, preferred_element_type=jnp.float32)
                total = term if total is None else total + term
        return total

    sends = pack(block_ids, live_mask, blocks, owners, owned)
    gots = []
    for send in sends:
        gots.append(lax.all_to_all(send, "pair", split_axis=0, concat_axis=0, tiled=True))
    results = []
    for c, got in enumerate(gots):
        halves = half_transform(me.reshape(1), gots[0], got, occ_coeffs, owned, width, occ)
        parts = [across(halves[j], j) for j in range(occ)]
        piece = jnp.concatenate(parts, axis=0) if occ > 1 else parts[0]
        results.append(second_half(*gather(piece, c == len(gots) - 1)))
    return place(me.reshape(1), results, occ, slab)


def solution(mesh):
    return jax.shard_map(
        on_device,
        mesh=mesh,
        in_specs=(
            P("pair", None, None, "occ"),
            P(),
            P(None, "pair"),
            P(None, "pair", None),
            P("pair", None),
        ),
        out_specs=P("occ", None, "pair"),
        check_vma=False,
    )
```

```python
import functools

import jax
import jax.numpy as jnp
from jax import lax
from jax.experimental import pallas as pl
from jax.experimental.pallas import tpu as pltpu
from jax.sharding import PartitionSpec as P


LIVE = 4
TAIL = 16
GRANT = 16 * 2**20


def pack_kernel(owned, ids_ref, live_ref, blocks_ref, *refs):
    out_refs = refs[:-2]
    pick_ref, sems = refs[-2:]
    owners, _, lanes = out_refs[0].shape
    width = blocks_ref.shape[1]
    group = live_ref.shape[1] // owners
    row = lax.broadcasted_iota(jnp.int32, (TAIL, 128), 0)
    lane = lax.broadcasted_iota(jnp.int32, (TAIL, 128), 1)

    def copy(owner, k, slot, c):
        return pltpu.make_async_copy(
            blocks_ref.at[slot, :, pl.ds(c * lanes, lanes)],
            out_refs[c].at[owner, pl.ds(k * width, width), :],
            sems.at[owner, k, c],
        )

    @pl.loop(0, owners)
    def _(owner):
        base = owner * group
        count = jnp.int32(0)
        for j in range(group):
            pick_ref[jnp.minimum(count, LIVE)] = base + j
            count = count + live_ref[0, base + j]
        tile = jnp.zeros((TAIL, 128), jnp.int32)
        for k in range(LIVE):
            slot = jnp.where(k < count, pick_ref[k], base)
            for c in range(len(out_refs)):
                copy(owner, k, slot, c).start()
            mu = ids_ref[0, 0, slot]
            nu = jnp.where(k < count, lax.rem(ids_ref[1, 0, slot], owned), owned)
            tile = jnp.where((row == 0) & (lane == k), mu, tile)
            tile = jnp.where((row == 0) & (lane == LIVE + k), nu, tile)
        out_refs[0][owner, LIVE * width :, :] = tile.astype(jnp.float32).astype(jnp.bfloat16)

    @pl.loop(0, owners)
    def _(owner):
        for k in range(LIVE):
            for c in range(len(out_refs)):
                copy(owner, k, 0, c).wait()


def pack(block_ids, live_mask, blocks, owners, owned):
    _, width, minor = blocks.shape
    chunks = minor // 128
    shapes = [
        jax.ShapeDtypeStruct((owners, LIVE * width + (0 if c else TAIL), 128), jnp.bfloat16)
        for c in range(chunks)
    ]
    return pl.pallas_call(
        functools.partial(pack_kernel, owned),
        out_shape=shapes,
        in_specs=[
            pl.BlockSpec(memory_space=pltpu.SMEM),
            pl.BlockSpec(memory_space=pltpu.SMEM),
            pl.BlockSpec(memory_space=pl.ANY),
        ],
        out_specs=[pl.BlockSpec(memory_space=pltpu.VMEM)] * chunks,
        scratch_shapes=[
            pltpu.SMEM((LIVE + 1,), jnp.int32),
            pltpu.SemaphoreType.DMA((owners, LIVE, chunks)),
        ],
        name="pack_live",
    )(block_ids, live_mask, pltpu.with_memory_space_constraint(blocks, pltpu.HBM))


def half_kernel(owned, width, me_ref, tail_ref, got_ref, coeff_ref, *refs):
    out_refs = refs[:-4]
    ids_vmem, ids_smem, total, sem = refs[-4:]
    owners = got_ref.shape[0]
    aux = got_ref.shape[2] // width
    for p in range(owners):
        ids_vmem[p : p + 1, :] = tail_ref[p, 0:1, :].astype(jnp.float32).astype(jnp.int32)
    ids = pltpu.make_async_copy(ids_vmem, ids_smem, sem)
    ids.start()
    total[...] = jnp.zeros_like(total)
    ids.wait()

    @pl.loop(0, owners)
    def _(p):
        for k in range(LIVE):
            mu = ids_smem[p, k]
            nu = ids_smem[p, LIVE + k]
            block = got_ref[p, k * width : (k + 1) * width, :]
            stacked = jnp.concatenate(
                [block[:, q * width : (q + 1) * width] for q in range(aux)], axis=0
            )
            coeff = coeff_ref[pl.ds(pl.multiple_of(mu * width, width), width), :]
            total[nu] += lax.dot_general(
                coeff, stacked, (((0,), (1,)), ((), ())), preferred_element_type=jnp.float32
            )

    slab = total.shape[1] // len(out_refs)
    for j, out_ref in enumerate(out_refs):
        start = pl.multiple_of((me_ref[0] ^ j) * slab, slab)
        for b in range(0, owned, 2):
            pair = [total[c, pl.ds(start, slab), :] for c in range(b, min(b + 2, owned))]
            for q in range(aux):
                cut = [t[:, q * width : (q + 1) * width] for t in pair]
                piece = cut[0] if len(cut) == 1 else jnp.concatenate(cut, axis=1)
                out_ref[q * slab : (q + 1) * slab, b * width : b * width + piece.shape[1]] = (
                    piece.astype(jnp.bfloat16)
                )


def half_transform(me, first, got, coeffs, owned, width, occ):
    owners, _, lanes = got.shape
    aux = lanes // width
    occ_count = coeffs.shape[1]
    shape = jax.ShapeDtypeStruct((aux * occ_count // occ, owned * width), jnp.bfloat16)
    vmem = pl.BlockSpec(memory_space=pltpu.VMEM)

    def whole(*dims):
        return pl.BlockSpec(dims, lambda g: (0,) * len(dims))

    return pl.pallas_call(
        functools.partial(half_kernel, owned, width),
        grid=(1,),
        out_shape=[shape] * occ,
        in_specs=[
            pl.BlockSpec(memory_space=pltpu.SMEM),
            pl.BlockSpec((owners, TAIL, lanes), lambda g: (0, LIVE * width // TAIL, 0)),
            pl.BlockSpec((owners, LIVE * width, lanes), lambda g: (0, 0, 0)),
            whole(*coeffs.shape),
        ],
        out_specs=[whole(*shape.shape)] * occ,
        scratch_shapes=[
            pltpu.VMEM((owners, lanes), jnp.int32),
            pltpu.SMEM((owners, lanes), jnp.int32),
            pltpu.VMEM((owned + 1, occ_count, lanes), jnp.float32),
            pltpu.SemaphoreType.DMA,
        ],
        cost_estimate=pl.CostEstimate(
            flops=2 * owners * LIVE * width * lanes * occ_count,
            bytes_accessed=2 * (got.size + coeffs.size + occ * shape.size),
            transcendentals=0,
        ),
        compiler_params=pltpu.CompilerParams(vmem_limit_bytes=GRANT),
        name="half_transform",
    )(me, first, got, pltpu.with_memory_space_constraint(coeffs, pltpu.HBM))


def place_kernel(occ, me_ref, *refs):
    in_refs, (out_ref, wide) = refs[:-2], refs[-2:]
    slab, aux, _ = out_ref.shape
    chunks = len(in_refs)
    local = aux // (occ * chunks)
    for c, in_ref in enumerate(in_refs):
        for j in range(occ):
            for q in range(local):
                at = (me_ref[0] ^ j) * (chunks * local) + c * local + q
                row = (j * local + q) * slab
                for t in range(wide.shape[0]):
                    wide[t, pl.ds(at, slab, stride=aux), :] = in_ref[
                        row : row + slab, t * 128 : (t + 1) * 128
                    ]
    for t in range(wide.shape[0]):
        out_ref[:, :, t * 128 : (t + 1) * 128] = (
            wide[t].reshape(slab, aux, 128).astype(out_ref.dtype)
        )


def place(me, parts, occ, slab):
    rows, columns = parts[0].shape
    aux = rows * len(parts) // slab
    vmem = pl.BlockSpec(memory_space=pltpu.VMEM)
    return pl.pallas_call(
        functools.partial(place_kernel, occ),
        out_shape=jax.ShapeDtypeStruct((slab, aux, columns), jnp.bfloat16),
        in_specs=[pl.BlockSpec(memory_space=pltpu.SMEM)] + [vmem] * len(parts),
        out_specs=vmem,
        scratch_shapes=[pltpu.VMEM((columns // 128, slab * aux, 128), jnp.float32)],
        compiler_params=pltpu.CompilerParams(vmem_limit_bytes=GRANT),
        name="place",
    )(me, *parts)


def on_device(integrals, occ_coeffs, virt_coeffs, block_ids, live_mask):
    blocks = integrals[0]
    width = blocks.shape[1]
    occ_count = occ_coeffs.shape[1]
    owners = lax.axis_size("pair")
    occ = lax.axis_size("occ")
    owned = occ_coeffs.shape[0] // width // owners
    slab = occ_count // occ
    outer = owners // 2
    rows = owned * width
    me = lax.axis_index("occ").astype(jnp.int32)
    here = lax.axis_index("pair")

    def across(array, j):
        if j == 0:
            return array
        return lax.ppermute(array, "occ", [(o, o ^ j) for o in range(occ)])

    def along(array):
        return lax.ppermute(
            array, "pair", [(p, (p // 2 + 1) % outer * 2 + p % 2) for p in range(owners)]
        )

    def swap(array):
        return lax.ppermute(array, "pair", [(p, p ^ 1) for p in range(owners)])

    def gather(piece, last):
        own, other = [piece], [swap(piece)]
        for shift in range(1, outer):
            own.append(along(own[-1]))
            if last and shift == outer - 1:
                other.append(along(other[-1]))
            else:
                other.append(swap(own[-1]))
        return own, other

    def second_half(own, other):
        total = None
        for shift in range(outer):
            for flip, array in enumerate((own[shift], other[shift])):
                source = (here // 2 - shift) % outer * 2 + (here % 2 ^ flip)
                part = lax.dynamic_slice_in_dim(virt_coeffs, source * rows, rows, axis=0)
                term = jnp.dot(array, part, preferred_element_type=jnp.float32)
                total = term if total is None else total + term
        return total

    sends = pack(block_ids, live_mask, blocks, owners, owned)
    gots = []
    for send in sends:
        gots.append(lax.all_to_all(send, "pair", split_axis=0, concat_axis=0, tiled=True))
    results = []
    for c, got in enumerate(gots):
        halves = half_transform(me.reshape(1), gots[0], got, occ_coeffs, owned, width, occ)
        parts = [across(halves[j], j) for j in range(occ)]
        piece = jnp.concatenate(parts, axis=0) if occ > 1 else parts[0]
        results.append(second_half(*gather(piece, c == len(gots) - 1)))
    return place(me.reshape(1), results, occ, slab)


def solution(mesh):
    return jax.shard_map(
        on_device,
        mesh=mesh,
        in_specs=(
            P("pair", None, None, "occ"),
            P(),
            P(None, "pair"),
            P(None, "pair", None),
            P("pair", None),
        ),
        out_specs=P("occ", None, "pair"),
        check_vma=False,
    )
```

```python
import functools

import jax
import jax.numpy as jnp
from jax import lax
from jax.experimental import pallas as pl
from jax.experimental.pallas import tpu as pltpu
from jax.sharding import PartitionSpec as P


LIVE = 4
TAIL = 16
GRANT = 16 * 2**20


def relative(here, k, owners, sign):
    outer = owners // 2
    return lax.rem(here // 2 + sign * (k // 2) + outer, outer) * 2 + lax.rem(here + k, 2)


def pack_kernel(owned, here_ref, ids_ref, live_ref, blocks_ref, first_ref, *refs):
    rest_refs = refs[:-2]
    pick_ref, sems = refs[-2:]
    owners, _, lanes = first_ref.shape
    width = blocks_ref.shape[1]
    group = live_ref.shape[1] // owners
    row = lax.broadcasted_iota(jnp.int32, (TAIL, 128), 0)
    lane = lax.broadcasted_iota(jnp.int32, (TAIL, 128), 1)

    def copies(owner, n, k, slot):
        block = blocks_ref.at[slot]
        rows = pl.ds(k * width, width)
        yield pltpu.make_async_copy(
            block.at[:, pl.ds(0, lanes)], first_ref.at[owner, rows, :], sems.at[n, k, 0]
        )
        for c in range(1, len(rest_refs) // owners + 1):
            yield pltpu.make_async_copy(
                block.at[:, pl.ds(c * lanes, lanes)],
                rest_refs[(c - 1) * owners + n].at[rows, :],
                sems.at[n, k, c],
            )

    for n in range(owners):
        owner = relative(here_ref[0], n, owners, 1)
        base = owner * group
        count = jnp.int32(0)
        for j in range(group):
            pick_ref[n, jnp.minimum(count, LIVE)] = base + j
            count = count + live_ref[0, base + j]
        tile = jnp.zeros((TAIL, 128), jnp.int32)
        for k in range(LIVE):
            slot = jnp.where(k < count, pick_ref[n, k], base)
            for copy in copies(owner, n, k, slot):
                copy.start()
            mu = ids_ref[0, 0, slot]
            nu = jnp.where(k < count, lax.rem(ids_ref[1, 0, slot], owned), owned)
            tile = jnp.where((row == 0) & (lane == k), mu, tile)
            tile = jnp.where((row == 0) & (lane == LIVE + k), nu, tile)
        first_ref[owner, LIVE * width :, :] = tile.astype(jnp.float32).astype(jnp.bfloat16)
    for n in range(owners):
        for k in range(LIVE):
            for copy in copies(relative(here_ref[0], n, owners, 1), n, k, 0):
                copy.wait()


def pack(here, block_ids, live_mask, blocks, owners, owned):
    _, width, minor = blocks.shape
    chunks = minor // 128
    shapes = [jax.ShapeDtypeStruct((owners, LIVE * width + TAIL, 128), jnp.bfloat16)]
    shapes += [jax.ShapeDtypeStruct((LIVE * width, 128), jnp.bfloat16)] * (
        owners * (chunks - 1)
    )
    smem = pl.BlockSpec(memory_space=pltpu.SMEM)
    return pl.pallas_call(
        functools.partial(pack_kernel, owned),
        out_shape=shapes,
        in_specs=[smem, smem, smem, pl.BlockSpec(memory_space=pl.ANY)],
        out_specs=[pl.BlockSpec(memory_space=pltpu.VMEM)] * len(shapes),
        scratch_shapes=[
            pltpu.SMEM((owners, LIVE + 1), jnp.int32),
            pltpu.SemaphoreType.DMA((owners, LIVE, chunks)),
        ],
        name="pack_live",
    )(here, block_ids, live_mask, pltpu.with_memory_space_constraint(blocks, pltpu.HBM))


def half_kernel(owned, width, rest, place_ref, tail_ref, coeff_ref, *refs):
    got_refs, refs = refs[:rest], refs[rest:]
    out_refs = refs[:-4]
    ids_vmem, ids_smem, total, sem = refs[-4:]
    owners, _, lanes = tail_ref.shape
    aux = lanes // width
    for p in range(owners):
        ids_vmem[p : p + 1, :] = tail_ref[p, 0:1, :].astype(jnp.float32).astype(jnp.int32)
    ids = pltpu.make_async_copy(ids_vmem, ids_smem, sem)
    ids.start()
    total[...] = jnp.zeros_like(total)
    ids.wait()

    def add(p, k, block):
        mu = ids_smem[p, k]
        nu = ids_smem[p, LIVE + k]
        stacked = jnp.concatenate(
            [block[:, q * width : (q + 1) * width] for q in range(aux)], axis=0
        )
        coeff = coeff_ref[pl.ds(pl.multiple_of(mu * width, width), width), :]
        total[nu] += lax.dot_general(
            coeff, stacked, (((0,), (1,)), ((), ())), preferred_element_type=jnp.float32
        )

    if rest > 1:
        for n, got_ref in enumerate(got_refs):
            p = relative(place_ref[1], n, owners, -1)
            for k in range(LIVE):
                add(p, k, got_ref[k * width : (k + 1) * width, :])
    else:

        @pl.loop(0, owners)
        def _(p):
            for k in range(LIVE):
                add(p, k, got_refs[0][p, k * width : (k + 1) * width, :])

    slab = total.shape[1] // len(out_refs)
    for j, out_ref in enumerate(out_refs):
        start = pl.multiple_of((place_ref[0] ^ j) * slab, slab)
        for b in range(0, owned, 2):
            pair = [total[c, pl.ds(start, slab), :] for c in range(b, min(b + 2, owned))]
            for q in range(aux):
                cut = [t[:, q * width : (q + 1) * width] for t in pair]
                piece = cut[0] if len(cut) == 1 else jnp.concatenate(cut, axis=1)
                out_ref[q * slab : (q + 1) * slab, b * width : b * width + piece.shape[1]] = (
                    piece.astype(jnp.bfloat16)
                )


def half_transform(place, first, gots, coeffs, owned, width, occ):
    owners, _, lanes = first.shape
    aux = lanes // width
    occ_count = coeffs.shape[1]
    shape = jax.ShapeDtypeStruct((aux * occ_count // occ, owned * width), jnp.bfloat16)

    def whole(*dims):
        return pl.BlockSpec(dims, lambda g: (0,) * len(dims))

    if len(gots) == 1:
        blocks = [whole(owners, LIVE * width, lanes)]
    else:
        blocks = [whole(*got.shape) for got in gots]
    return pl.pallas_call(
        functools.partial(half_kernel, owned, width, len(gots)),
        grid=(1,),
        out_shape=[shape] * occ,
        in_specs=[
            pl.BlockSpec(memory_space=pltpu.SMEM),
            pl.BlockSpec((owners, TAIL, lanes), lambda g: (0, LIVE * width // TAIL, 0)),
            whole(*coeffs.shape),
            *blocks,
        ],
        out_specs=[whole(*shape.shape)] * occ,
        scratch_shapes=[
            pltpu.VMEM((owners, lanes), jnp.int32),
            pltpu.SMEM((owners, lanes), jnp.int32),
            pltpu.VMEM((owned + 1, occ_count, lanes), jnp.float32),
            pltpu.SemaphoreType.DMA,
        ],
        cost_estimate=pl.CostEstimate(
            flops=2 * owners * LIVE * width * lanes * occ_count,
            bytes_accessed=2 * (first.size + coeffs.size + occ * shape.size),
            transcendentals=0,
        ),
        compiler_params=pltpu.CompilerParams(vmem_limit_bytes=GRANT),
        name="half_transform",
    )(place, first, pltpu.with_memory_space_constraint(coeffs, pltpu.HBM), *gots)


def place_kernel(occ, me_ref, *refs):
    in_refs, (out_ref, wide) = refs[:-2], refs[-2:]
    slab, aux, _ = out_ref.shape
    chunks = len(in_refs)
    local = aux // (occ * chunks)
    for c, in_ref in enumerate(in_refs):
        for j in range(occ):
            for q in range(local):
                at = (me_ref[0] ^ j) * (chunks * local) + c * local + q
                row = (j * local + q) * slab
                for t in range(wide.shape[0]):
                    wide[t, pl.ds(at, slab, stride=aux), :] = in_ref[
                        row : row + slab, t * 128 : (t + 1) * 128
                    ]
    for t in range(wide.shape[0]):
        out_ref[:, :, t * 128 : (t + 1) * 128] = (
            wide[t].reshape(slab, aux, 128).astype(out_ref.dtype)
        )


def place(me, parts, occ, slab):
    rows, columns = parts[0].shape
    aux = rows * len(parts) // slab
    vmem = pl.BlockSpec(memory_space=pltpu.VMEM)
    return pl.pallas_call(
        functools.partial(place_kernel, occ),
        out_shape=jax.ShapeDtypeStruct((slab, aux, columns), jnp.bfloat16),
        in_specs=[pl.BlockSpec(memory_space=pltpu.SMEM)] + [vmem] * len(parts),
        out_specs=vmem,
        scratch_shapes=[pltpu.VMEM((columns // 128, slab * aux, 128), jnp.float32)],
        compiler_params=pltpu.CompilerParams(vmem_limit_bytes=GRANT),
        name="place",
    )(me, *parts)


def on_device(integrals, occ_coeffs, virt_coeffs, block_ids, live_mask):
    blocks = integrals[0]
    width = blocks.shape[1]
    occ_count = occ_coeffs.shape[1]
    owners = lax.axis_size("pair")
    occ = lax.axis_size("occ")
    owned = occ_coeffs.shape[0] // width // owners
    slab = occ_count // occ
    outer = owners // 2
    rows = owned * width
    me = lax.axis_index("occ").astype(jnp.int32)
    here = lax.axis_index("pair")

    def across(array, j):
        if j == 0:
            return array
        return lax.ppermute(array, "occ", [(o, o ^ j) for o in range(occ)])

    def along(array):
        return lax.ppermute(
            array, "pair", [(p, (p // 2 + 1) % outer * 2 + p % 2) for p in range(owners)]
        )

    def swap(array):
        return lax.ppermute(array, "pair", [(p, p ^ 1) for p in range(owners)])

    def gather(piece, last):
        own, other = [piece], [swap(piece)]
        for shift in range(1, outer):
            own.append(along(own[-1]))
            if last and shift == outer - 1:
                other.append(along(other[-1]))
            else:
                other.append(swap(own[-1]))
        return own, other

    def second_half(own, other):
        total = None
        for shift in range(outer):
            for flip, array in enumerate((own[shift], other[shift])):
                source = (here // 2 - shift) % outer * 2 + (here % 2 ^ flip)
                part = lax.dynamic_slice_in_dim(virt_coeffs, source * rows, rows, axis=0)
                term = jnp.dot(array, part, preferred_element_type=jnp.float32)
                total = term if total is None else total + term
        return total

    spot = jnp.stack([me, here.astype(jnp.int32)])
    sends = pack(spot[1:], block_ids, live_mask, blocks, owners, owned)
    first = lax.all_to_all(sends[0], "pair", split_axis=0, concat_axis=0, tiled=True)
    gots = [[first]]
    for c in range(1, 1 + len(sends[1:]) // owners):
        mine = sends[1 + (c - 1) * owners : 1 + c * owners]
        got = [pltpu.with_memory_space_constraint(mine[0], pltpu.HBM)]
        for n in range(1, owners):
            target = [
                (p, (p // 2 + n // 2) % outer * 2 + (p + n) % 2) for p in range(owners)
            ]
            got.append(lax.ppermute(mine[n], "pair", target))
        gots.append(got)
    results = []
    for c, got in enumerate(gots):
        halves = half_transform(spot, first, got, occ_coeffs, owned, width, occ)
        parts = [across(halves[j], j) for j in range(occ)]
        piece = jnp.concatenate(parts, axis=0) if occ > 1 else parts[0]
        results.append(second_half(*gather(piece, c == len(gots) - 1)))
    return place(me.reshape(1), results, occ, slab)


def solution(mesh):
    return jax.shard_map(
        on_device,
        mesh=mesh,
        in_specs=(
            P("pair", None, None, "occ"),
            P(),
            P(None, "pair"),
            P(None, "pair", None),
            P("pair", None),
        ),
        out_specs=P("occ", None, "pair"),
        check_vma=False,
    )
```

```python
import functools

import jax
import jax.numpy as jnp
from jax import lax
from jax.experimental import pallas as pl
from jax.experimental.pallas import tpu as pltpu
from jax.sharding import PartitionSpec as P


LIVE = 4
TAIL = 16
GRANT = 16 * 2**20


def relative(here, n, owners):
    outer = owners // 2
    return lax.rem(here // 2 + n // 2, outer) * 2 + lax.rem(here + n, 2)


def pack_kernel(owned, here_ref, ids_ref, live_ref, blocks_ref, *refs):
    out_refs = refs[:-2]
    pick_ref, sems = refs[-2:]
    owners = pick_ref.shape[0]
    lanes = out_refs[0].shape[1]
    width = blocks_ref.shape[1]
    group = live_ref.shape[1] // owners
    row = lax.broadcasted_iota(jnp.int32, (TAIL, 128), 0)
    lane = lax.broadcasted_iota(jnp.int32, (TAIL, 128), 1)

    def copies(n, k, slot):
        for c in range(len(out_refs) // owners):
            yield pltpu.make_async_copy(
                blocks_ref.at[slot, :, pl.ds(c * lanes, lanes)],
                out_refs[c * owners + n].at[pl.ds(k * width, width), :],
                sems.at[n, k, c],
            )

    for n in range(owners):
        base = relative(here_ref[0], n, owners) * group
        count = jnp.int32(0)
        for j in range(group):
            pick_ref[n, jnp.minimum(count, LIVE)] = base + j
            count = count + live_ref[0, base + j]
        tile = jnp.zeros((TAIL, 128), jnp.int32)
        for k in range(LIVE):
            slot = jnp.where(k < count, pick_ref[n, k], base)
            for copy in copies(n, k, slot):
                copy.start()
            mu = ids_ref[0, 0, slot]
            nu = jnp.where(k < count, lax.rem(ids_ref[1, 0, slot], owned), owned)
            tile = jnp.where((row == 0) & (lane == k), mu, tile)
            tile = jnp.where((row == 0) & (lane == LIVE + k), nu, tile)
        out_refs[n][LIVE * width :, :] = tile.astype(jnp.float32).astype(jnp.bfloat16)
    for n in range(owners):
        for k in range(LIVE):
            for copy in copies(n, k, 0):
                copy.wait()


def pack(here, block_ids, live_mask, blocks, owners, owned):
    _, width, minor = blocks.shape
    chunks = minor // 128
    shapes = [
        jax.ShapeDtypeStruct((LIVE * width + (0 if c else TAIL), 128), jnp.bfloat16)
        for c in range(chunks)
        for _ in range(owners)
    ]
    smem = pl.BlockSpec(memory_space=pltpu.SMEM)
    return pl.pallas_call(
        functools.partial(pack_kernel, owned),
        out_shape=shapes,
        in_specs=[smem, smem, smem, pl.BlockSpec(memory_space=pl.ANY)],
        out_specs=[pl.BlockSpec(memory_space=pltpu.VMEM)] * len(shapes),
        scratch_shapes=[
            pltpu.SMEM((owners, LIVE + 1), jnp.int32),
            pltpu.SemaphoreType.DMA((owners, LIVE, chunks)),
        ],
        name="pack_live",
    )(here, block_ids, live_mask, pltpu.with_memory_space_constraint(blocks, pltpu.HBM))


def half_kernel(owned, width, owners, me_ref, *refs):
    refs = list(refs)
    given = refs.pop(0) if refs[0].dtype == jnp.int32 else None
    coeff_ref = refs.pop(0)
    got_refs, refs = refs[:owners], refs[owners:]
    if given is None:
        total, ids_smem, sem = refs[-3:]
        out_refs, ids_vmem = refs[:-4], refs[-4]
        for n, got_ref in enumerate(got_refs):
            ids_vmem[n : n + 1, :] = (
                got_ref[LIVE * width :, :][0:1].astype(jnp.float32).astype(jnp.int32)
            )
        ids = pltpu.make_async_copy(ids_vmem, ids_smem, sem)
        ids.start()
        total[...] = jnp.zeros_like(total)
        ids.wait()
    else:
        ids_smem, out_refs, total = given, refs[:-1], refs[-1]
        total[...] = jnp.zeros_like(total)
    aux = got_refs[0].shape[1] // width
    for n, got_ref in enumerate(got_refs):
        for k in range(LIVE):
            mu = ids_smem[n, k]
            nu = ids_smem[n, LIVE + k]
            block = got_ref[k * width : (k + 1) * width, :]
            stacked = jnp.concatenate(
                [block[:, q * width : (q + 1) * width] for q in range(aux)], axis=0
            )
            total[nu] += lax.dot_general(
                coeff_ref[mu], stacked, (((1,), (1,)), ((), ())), preferred_element_type=jnp.float32
            )

    slab = total.shape[1] // len(out_refs)
    for j, out_ref in enumerate(out_refs):
        start = pl.multiple_of((me_ref[0] ^ j) * slab, slab)
        for b in range(0, owned, 2):
            pair = [total[c, pl.ds(start, slab), :] for c in range(b, min(b + 2, owned))]
            for q in range(aux):
                cut = [t[:, q * width : (q + 1) * width] for t in pair]
                piece = cut[0] if len(cut) == 1 else jnp.concatenate(cut, axis=1)
                out_ref[q * slab : (q + 1) * slab, b * width : b * width + piece.shape[1]] = (
                    piece.astype(jnp.bfloat16)
                )


def half_transform(me, ids, gots, coeffs, owned, width, occ):
    owners = len(gots)
    lanes = gots[0].shape[1]
    aux = lanes // width
    occ_count = coeffs.shape[1]
    assert coeffs.shape[2] == width
    shape = jax.ShapeDtypeStruct((aux * occ_count // occ, owned * width), jnp.bfloat16)
    smem = pl.BlockSpec(memory_space=pltpu.SMEM)
    vmem = pl.BlockSpec(memory_space=pltpu.VMEM)
    shapes = [shape] * occ
    scratch = [pltpu.VMEM((owned + 1, occ_count, lanes), jnp.float32)]
    if ids is None:
        shapes.append(jax.ShapeDtypeStruct((owners, lanes), jnp.int32))
        scratch += [pltpu.SMEM((owners, lanes), jnp.int32), pltpu.SemaphoreType.DMA]
    result = pl.pallas_call(
        functools.partial(half_kernel, owned, width, owners),
        out_shape=shapes,
        in_specs=[smem] + ([] if ids is None else [smem]) + [vmem] * (1 + owners),
        out_specs=[vmem] * len(shapes),
        scratch_shapes=scratch,
        cost_estimate=pl.CostEstimate(
            flops=2 * owners * LIVE * width * lanes * occ_count,
            bytes_accessed=2 * (owners * gots[0].size + coeffs.size + occ * shape.size),
            transcendentals=0,
        ),
        compiler_params=pltpu.CompilerParams(vmem_limit_bytes=GRANT),
        name="half_transform",
    )(me, *([] if ids is None else [ids]), coeffs, *gots)
    return result[:occ], result[occ] if ids is None else ids


def place_kernel(occ, me_ref, *refs):
    in_refs, (out_ref, wide) = refs[:-2], refs[-2:]
    slab, aux, _ = out_ref.shape
    chunks = len(in_refs)
    local = aux // (occ * chunks)
    for c, in_ref in enumerate(in_refs):
        for j in range(occ):
            for q in range(local):
                at = (me_ref[0] ^ j) * (chunks * local) + c * local + q
                row = (j * local + q) * slab
                for t in range(wide.shape[0]):
                    wide[t, pl.ds(at, slab, stride=aux), :] = in_ref[
                        row : row + slab, t * 128 : (t + 1) * 128
                    ]
    for t in range(wide.shape[0]):
        out_ref[:, :, t * 128 : (t + 1) * 128] = (
            wide[t].reshape(slab, aux, 128).astype(out_ref.dtype)
        )


def place(me, parts, occ, slab):
    rows, columns = parts[0].shape
    aux = rows * len(parts) // slab
    vmem = pl.BlockSpec(memory_space=pltpu.VMEM)
    return pl.pallas_call(
        functools.partial(place_kernel, occ),
        out_shape=jax.ShapeDtypeStruct((slab, aux, columns), jnp.bfloat16),
        in_specs=[pl.BlockSpec(memory_space=pltpu.SMEM)] + [vmem] * len(parts),
        out_specs=vmem,
        scratch_shapes=[pltpu.VMEM((columns // 128, slab * aux, 128), jnp.float32)],
        compiler_params=pltpu.CompilerParams(vmem_limit_bytes=GRANT),
        name="place",
    )(me, *parts)


def on_device(integrals, occ_coeffs, virt_coeffs, block_ids, live_mask):
    blocks = integrals[0]
    width = blocks.shape[1]
    occ_count = occ_coeffs.shape[1]
    owners = lax.axis_size("pair")
    occ = lax.axis_size("occ")
    owned = occ_coeffs.shape[0] // width // owners
    slab = occ_count // occ
    outer = owners // 2
    rows = owned * width
    me = lax.axis_index("occ").astype(jnp.int32)
    here = lax.axis_index("pair")

    def across(array, j):
        if j == 0:
            return array
        return lax.ppermute(array, "occ", [(o, o ^ j) for o in range(occ)])

    def along(array):
        return lax.ppermute(
            array, "pair", [(p, (p // 2 + 1) % outer * 2 + p % 2) for p in range(owners)]
        )

    def swap(array):
        return lax.ppermute(array, "pair", [(p, p ^ 1) for p in range(owners)])

    def gather(piece, last):
        own, other = [piece], [swap(piece)]
        for shift in range(1, outer):
            own.append(along(own[-1]))
            if last and shift == outer - 1:
                other.append(along(other[-1]))
            else:
                other.append(swap(own[-1]))
        return own, other

    def second_half(own, other):
        total = None
        for shift in range(outer):
            for flip, array in enumerate((own[shift], other[shift])):
                source = (here // 2 - shift) % outer * 2 + (here % 2 ^ flip)
                part = lax.dynamic_slice_in_dim(virt_coeffs, source * rows, rows, axis=0)
                term = jnp.dot(array, part, preferred_element_type=jnp.float32)
                total = term if total is None else total + term
        return total

    sends = pack(here.astype(jnp.int32).reshape(1), block_ids, live_mask, blocks, owners, owned)
    gots = []
    for c in range(len(sends) // owners):
        mine = sends[c * owners : (c + 1) * owners]
        got = [pltpu.with_memory_space_constraint(mine[0], pltpu.HBM)]
        for n in range(1, owners):
            target = [
                (p, (p // 2 + n // 2) % outer * 2 + (p + n) % 2) for p in range(owners)
            ]
            got.append(lax.ppermute(mine[n], "pair", target))
        gots.append(got)
    coeffs = occ_coeffs.reshape(-1, width, occ_count).transpose(0, 2, 1)
    results, ids = [], None
    for c, got in enumerate(gots):
        halves, ids = half_transform(
            me.reshape(1), ids, got, coeffs, owned, width, occ
        )
        parts = [across(halves[j], j) for j in range(occ)]
        piece = jnp.concatenate(parts, axis=0) if occ > 1 else parts[0]
        results.append(second_half(*gather(piece, c == len(gots) - 1)))
    return place(me.reshape(1), results, occ, slab)


def solution(mesh):
    return jax.shard_map(
        on_device,
        mesh=mesh,
        in_specs=(
            P("pair", None, None, "occ"),
            P(),
            P(None, "pair"),
            P(None, "pair", None),
            P("pair", None),
        ),
        out_specs=P("occ", None, "pair"),
        check_vma=False,
    )
```

```python
import functools

import jax
import jax.numpy as jnp
from jax import lax
from jax.experimental import pallas as pl
from jax.experimental.pallas import tpu as pltpu
from jax.sharding import PartitionSpec as P


LIVE = 4
TAIL = 16
GRANT = 16 * 2**20


def relative(here, n, owners, sign=1):
    outer = owners // 2
    return lax.rem(here // 2 + sign * (n // 2) + outer, outer) * 2 + lax.rem(here + n, 2)


def pack_kernel(owned, here_ref, ids_ref, live_ref, blocks_ref, *refs):
    out_refs = refs[:-2]
    pick_ref, sems = refs[-2:]
    owners = pick_ref.shape[0]
    lanes = out_refs[0].shape[1]
    width = blocks_ref.shape[1]
    group = live_ref.shape[1] // owners
    row = lax.broadcasted_iota(jnp.int32, (TAIL, 128), 0)
    lane = lax.broadcasted_iota(jnp.int32, (TAIL, 128), 1)

    def copies(n, k, slot):
        owner = relative(here_ref[0], n, owners)
        for c in range(1 + len(out_refs) - owners):
            out = out_refs[owners + c - 1].at[owner] if c else out_refs[n]
            yield pltpu.make_async_copy(
                blocks_ref.at[slot, :, pl.ds(c * lanes, lanes)],
                out.at[pl.ds(k * width, width), :],
                sems.at[n, k, c],
            )

    for n in range(owners):
        base = relative(here_ref[0], n, owners) * group
        count = jnp.int32(0)
        for j in range(group):
            pick_ref[n, jnp.minimum(count, LIVE)] = base + j
            count = count + live_ref[0, base + j]
        tile = jnp.zeros((TAIL, 128), jnp.int32)
        for k in range(LIVE):
            slot = jnp.where(k < count, pick_ref[n, k], base)
            for copy in copies(n, k, slot):
                copy.start()
            mu = ids_ref[0, 0, slot]
            nu = jnp.where(k < count, lax.rem(ids_ref[1, 0, slot], owned), owned)
            tile = jnp.where((row == 0) & (lane == k), mu, tile)
            tile = jnp.where((row == 0) & (lane == LIVE + k), nu, tile)
        out_refs[n][LIVE * width :, :] = tile.astype(jnp.float32).astype(jnp.bfloat16)
    for n in range(owners):
        for k in range(LIVE):
            for copy in copies(n, k, 0):
                copy.wait()


def pack(here, block_ids, live_mask, blocks, owners, owned):
    _, width, minor = blocks.shape
    chunks = minor // 128
    shapes = [jax.ShapeDtypeStruct((LIVE * width + TAIL, 128), jnp.bfloat16)] * owners
    shapes += [jax.ShapeDtypeStruct((owners, LIVE * width, 128), jnp.bfloat16)] * (chunks - 1)
    smem = pl.BlockSpec(memory_space=pltpu.SMEM)
    return pl.pallas_call(
        functools.partial(pack_kernel, owned),
        out_shape=shapes,
        in_specs=[smem, smem, smem, pl.BlockSpec(memory_space=pl.ANY)],
        out_specs=[pl.BlockSpec(memory_space=pltpu.VMEM)] * len(shapes),
        scratch_shapes=[
            pltpu.SMEM((owners, LIVE + 1), jnp.int32),
            pltpu.SemaphoreType.DMA((owners, LIVE, chunks)),
        ],
        compiler_params=pltpu.CompilerParams(vmem_limit_bytes=GRANT),
        name="pack_live",
    )(here, *(pltpu.with_memory_space_constraint(x, pltpu.HBM) for x in (block_ids, live_mask, blocks)))


def half_kernel(owned, width, owners, place_ref, *refs):
    refs = list(refs)
    given = refs.pop(0) if refs[0].dtype == jnp.int32 else None
    coeff_ref = refs.pop(0)
    if given is None:
        got_refs, refs = refs[:owners], refs[owners:]
        total, ids_smem, sem = refs[-3:]
        out_refs, ids_vmem = refs[:-4], refs[-4]
        for n, got_ref in enumerate(got_refs):
            ids_vmem[n : n + 1, :] = (
                got_ref[LIVE * width :, :][0:1].astype(jnp.float32).astype(jnp.int32)
            )
        ids = pltpu.make_async_copy(ids_vmem, ids_smem, sem)
        ids.start()
        total[...] = jnp.zeros_like(total)
        ids.wait()
    else:
        got_ref, ids_smem, out_refs, total = refs[0], given, refs[1:-1], refs[-1]
        got_refs = [got_ref.at[relative(place_ref[1], n, owners, -1)] for n in range(owners)]
        total[...] = jnp.zeros_like(total)
    aux = got_refs[0].shape[1] // width
    for n, got_ref in enumerate(got_refs):
        for k in range(LIVE):
            mu = ids_smem[n, k]
            nu = ids_smem[n, LIVE + k]
            block = got_ref[k * width : (k + 1) * width, :]
            stacked = jnp.concatenate(
                [block[:, q * width : (q + 1) * width] for q in range(aux)], axis=0
            )
            total[nu] += lax.dot_general(
                coeff_ref[mu], stacked, (((1,), (1,)), ((), ())), preferred_element_type=jnp.float32
            )

    slab = total.shape[1] // len(out_refs)
    for j, out_ref in enumerate(out_refs):
        start = pl.multiple_of((place_ref[0] ^ j) * slab, slab)
        for b in range(0, owned, 2):
            pair = [total[c, pl.ds(start, slab), :] for c in range(b, min(b + 2, owned))]
            for q in range(aux):
                cut = [t[:, q * width : (q + 1) * width] for t in pair]
                piece = cut[0] if len(cut) == 1 else jnp.concatenate(cut, axis=1)
                out_ref[q * slab : (q + 1) * slab, b * width : b * width + piece.shape[1]] = (
                    piece.astype(jnp.bfloat16)
                )


def half_transform(place, ids, gots, coeffs, owners, owned, width, occ):
    lanes = gots[0].shape[-1]
    aux = lanes // width
    occ_count = coeffs.shape[1]
    assert coeffs.shape[2] == width
    shape = jax.ShapeDtypeStruct((aux * occ_count // occ, owned * width), jnp.bfloat16)
    smem = pl.BlockSpec(memory_space=pltpu.SMEM)
    vmem = pl.BlockSpec(memory_space=pltpu.VMEM)
    shapes = [shape] * occ
    scratch = [pltpu.VMEM((owned + 1, occ_count, lanes), jnp.float32)]
    if ids is None:
        shapes.append(jax.ShapeDtypeStruct((owners, lanes), jnp.int32))
        scratch += [pltpu.SMEM((owners, lanes), jnp.int32), pltpu.SemaphoreType.DMA]
    result = pl.pallas_call(
        functools.partial(half_kernel, owned, width, owners),
        out_shape=shapes,
        in_specs=[smem] + ([] if ids is None else [smem]) + [vmem] * (1 + len(gots)),
        out_specs=[vmem] * len(shapes),
        scratch_shapes=scratch,
        cost_estimate=pl.CostEstimate(
            flops=2 * owners * LIVE * width * lanes * occ_count,
            bytes_accessed=2 * (len(gots) * gots[0].size + coeffs.size + occ * shape.size),
            transcendentals=0,
        ),
        compiler_params=pltpu.CompilerParams(vmem_limit_bytes=GRANT),
        name="half_transform",
    )(place, *([] if ids is None else [ids]), coeffs, *gots)
    return result[:occ], result[occ] if ids is None else ids


def place_kernel(occ, me_ref, *refs):
    in_refs, (out_ref, wide) = refs[:-2], refs[-2:]
    slab, aux, _ = out_ref.shape
    chunks = len(in_refs)
    local = aux // (occ * chunks)
    for c, in_ref in enumerate(in_refs):
        for j in range(occ):
            for q in range(local):
                at = (me_ref[0] ^ j) * (chunks * local) + c * local + q
                row = (j * local + q) * slab
                for t in range(wide.shape[0]):
                    wide[t, pl.ds(at, slab, stride=aux), :] = in_ref[
                        row : row + slab, t * 128 : (t + 1) * 128
                    ]
    for t in range(wide.shape[0]):
        out_ref[:, :, t * 128 : (t + 1) * 128] = (
            wide[t].reshape(slab, aux, 128).astype(out_ref.dtype)
        )


def place(me, parts, occ, slab):
    rows, columns = parts[0].shape
    aux = rows * len(parts) // slab
    vmem = pl.BlockSpec(memory_space=pltpu.VMEM)
    return pl.pallas_call(
        functools.partial(place_kernel, occ),
        out_shape=jax.ShapeDtypeStruct((slab, aux, columns), jnp.bfloat16),
        in_specs=[pl.BlockSpec(memory_space=pltpu.SMEM)] + [vmem] * len(parts),
        out_specs=vmem,
        scratch_shapes=[pltpu.VMEM((columns // 128, slab * aux, 128), jnp.float32)],
        compiler_params=pltpu.CompilerParams(vmem_limit_bytes=GRANT),
        name="place",
    )(me, *parts)


def on_device(integrals, occ_coeffs, virt_coeffs, block_ids, live_mask):
    blocks = integrals[0]
    width = blocks.shape[1]
    occ_count = occ_coeffs.shape[1]
    owners = lax.axis_size("pair")
    occ = lax.axis_size("occ")
    owned = occ_coeffs.shape[0] // width // owners
    slab = occ_count // occ
    outer = owners // 2
    rows = owned * width
    me = lax.axis_index("occ").astype(jnp.int32)
    here = lax.axis_index("pair")

    def across(array, j):
        if j == 0:
            return array
        return lax.ppermute(array, "occ", [(o, o ^ j) for o in range(occ)])

    def along(array):
        return lax.ppermute(
            array, "pair", [(p, (p // 2 + 1) % outer * 2 + p % 2) for p in range(owners)]
        )

    def swap(array):
        return lax.ppermute(array, "pair", [(p, p ^ 1) for p in range(owners)])

    def gather(piece, last):
        own, other = [piece], [swap(piece)]
        for shift in range(1, outer):
            own.append(along(own[-1]))
            if last and shift == outer - 1:
                other.append(along(other[-1]))
            else:
                other.append(swap(own[-1]))
        return own, other

    def second_half(own, other):
        total = None
        for shift in range(outer):
            for flip, array in enumerate((own[shift], other[shift])):
                source = (here // 2 - shift) % outer * 2 + (here % 2 ^ flip)
                part = lax.dynamic_slice_in_dim(virt_coeffs, source * rows, rows, axis=0)
                term = jnp.dot(array, part, preferred_element_type=jnp.float32)
                total = term if total is None else total + term
        return total

    sends = pack(here.astype(jnp.int32).reshape(1), block_ids, live_mask, blocks, owners, owned)
    got = [sends[0]]
    for n in range(1, owners):
        target = [(p, (p // 2 + n // 2) % outer * 2 + (p + n) % 2) for p in range(owners)]
        got.append(lax.ppermute(sends[n], "pair", target))
    gots = [got]
    for c, send in enumerate(sends[owners:], 1):
        gots.append([lax.all_to_all(send, "pair", split_axis=0, concat_axis=0, tiled=True)])
    spot = jnp.stack([me, here.astype(jnp.int32)])
    coeffs = occ_coeffs.reshape(-1, width, occ_count).transpose(0, 2, 1)
    results, ids = [], None
    for c, got in enumerate(gots):
        halves, ids = half_transform(
            spot, ids, got, coeffs, owners, owned, width, occ
        )
        parts = [across(halves[j], j) for j in range(occ)]
        piece = jnp.concatenate(parts, axis=0) if occ > 1 else parts[0]
        results.append(second_half(*gather(piece, c == len(gots) - 1)))
    return place(me.reshape(1), results, occ, slab)


def solution(mesh):
    return jax.shard_map(
        on_device,
        mesh=mesh,
        in_specs=(
            P("pair", None, None, "occ"),
            P(),
            P(None, "pair"),
            P(None, "pair", None),
            P("pair", None),
        ),
        out_specs=P("occ", None, "pair"),
        check_vma=False,
    )
```

```python
import functools

import jax
import jax.numpy as jnp
from jax import lax
from jax.experimental import pallas as pl
from jax.experimental.pallas import tpu as pltpu
from jax.sharding import PartitionSpec as P


LIVE = 4
TAIL = 16
GRANT = 16 * 2**20


def relative(here, n, owners, sign=1):
    outer = owners // 2
    return lax.rem(here // 2 + sign * (n // 2) + outer, outer) * 2 + lax.rem(here + n, 2)


def pack_kernel(owned, here_ref, ids_ref, live_ref, blocks_ref, *refs):
    out_refs = refs[:-2]
    pick_ref, sems = refs[-2:]
    owners = pick_ref.shape[0]
    lanes = out_refs[0].shape[1]
    width = blocks_ref.shape[1]
    group = live_ref.shape[1] // owners
    row = lax.broadcasted_iota(jnp.int32, (TAIL, 128), 0)
    lane = lax.broadcasted_iota(jnp.int32, (TAIL, 128), 1)

    def copies(n, k, slot):
        owner = relative(here_ref[0], n, owners)
        for c in range(1 + len(out_refs) - owners):
            out = out_refs[owners + c - 1].at[owner] if c else out_refs[n]
            yield pltpu.make_async_copy(
                blocks_ref.at[slot, :, pl.ds(c * lanes, lanes)],
                out.at[pl.ds(k * width, width), :],
                sems.at[n, k, c],
            )

    for n in range(owners):
        base = relative(here_ref[0], n, owners) * group
        count = jnp.int32(0)
        for j in range(group):
            pick_ref[n, jnp.minimum(count, LIVE)] = base + j
            count = count + live_ref[0, base + j]
        tile = jnp.zeros((TAIL, 128), jnp.int32)
        for k in range(LIVE):
            slot = jnp.where(k < count, pick_ref[n, k], base)
            for copy in copies(n, k, slot):
                copy.start()
            mu = ids_ref[0, 0, slot]
            nu = jnp.where(k < count, lax.rem(ids_ref[1, 0, slot], owned), owned)
            tile = jnp.where((row == 0) & (lane == k), mu, tile)
            tile = jnp.where((row == 0) & (lane == LIVE + k), nu, tile)
        out_refs[n][LIVE * width :, :] = tile.astype(jnp.float32).astype(jnp.bfloat16)
    for n in range(owners):
        for k in range(LIVE):
            for copy in copies(n, k, 0):
                copy.wait()


def pack(here, block_ids, live_mask, blocks, owners, owned):
    _, width, minor = blocks.shape
    chunks = minor // 128
    shapes = [jax.ShapeDtypeStruct((LIVE * width + TAIL, 128), jnp.bfloat16)] * owners
    shapes += [jax.ShapeDtypeStruct((owners, LIVE * width, 128), jnp.bfloat16)] * (chunks - 1)
    smem = pl.BlockSpec(memory_space=pltpu.SMEM)
    return pl.pallas_call(
        functools.partial(pack_kernel, owned),
        out_shape=shapes,
        in_specs=[smem, smem, smem, pl.BlockSpec(memory_space=pl.ANY)],
        out_specs=[pl.BlockSpec(memory_space=pltpu.VMEM)] * len(shapes),
        scratch_shapes=[
            pltpu.SMEM((owners, LIVE + 1), jnp.int32),
            pltpu.SemaphoreType.DMA((owners, LIVE, chunks)),
        ],
        name="pack_live",
    )(here, block_ids, live_mask, pltpu.with_memory_space_constraint(blocks, pltpu.HBM))


def half_kernel(owned, width, owners, place_ref, *refs):
    refs = list(refs)
    given = refs.pop(0) if refs[0].dtype == jnp.int32 else None
    coeff_ref = refs.pop(0)
    if given is None:
        got_refs, refs = refs[:owners], refs[owners:]
        total, ids_smem, sem = refs[-3:]
        out_refs, ids_vmem = refs[:-4], refs[-4]
        for n, got_ref in enumerate(got_refs):
            ids_vmem[n : n + 1, :] = (
                got_ref[LIVE * width :, :][0:1].astype(jnp.float32).astype(jnp.int32)
            )
        ids = pltpu.make_async_copy(ids_vmem, ids_smem, sem)
        ids.start()
        total[...] = jnp.zeros_like(total)
        ids.wait()
    else:
        got_ref, ids_smem, out_refs, total = refs[0], given, refs[1:-1], refs[-1]
        got_refs = [got_ref.at[relative(place_ref[1], n, owners, -1)] for n in range(owners)]
        total[...] = jnp.zeros_like(total)
    aux = got_refs[0].shape[1] // width
    low = lax.broadcasted_iota(jnp.int32, (width, 2 * width), 1) < width
    high = lax.broadcasted_iota(jnp.int32, (total.shape[1], 2 * width), 1) // width
    for n, got_ref in enumerate(got_refs):
        for k in range(LIVE):
            mu = ids_smem[n, k]
            nu = ids_smem[n, LIVE + k]
            block = got_ref[k * width : (k + 1) * width, :]
            turned = pltpu.roll(block.astype(jnp.float32), width, 1).astype(block.dtype)
            stacked = jnp.concatenate(
                [jnp.where(low, block, turned), jnp.where(low, turned, block)], axis=0
            )
            coeff = coeff_ref[mu // 2]
            coeff = jnp.where((high ^ lax.rem(mu, 2)) == 0, coeff, jnp.zeros_like(coeff))
            total[nu] += lax.dot_general(
                coeff, stacked, (((1,), (1,)), ((), ())), preferred_element_type=jnp.float32
            )

    slab = total.shape[1] // len(out_refs)
    for j, out_ref in enumerate(out_refs):
        start = pl.multiple_of((place_ref[0] ^ j) * slab, slab)
        for b in range(0, owned, 2):
            pair = [total[c, pl.ds(start, slab), :] for c in range(b, min(b + 2, owned))]
            for q in range(aux):
                cut = [t[:, q * width : (q + 1) * width] for t in pair]
                piece = cut[0] if len(cut) == 1 else jnp.concatenate(cut, axis=1)
                out_ref[q * slab : (q + 1) * slab, b * width : b * width + piece.shape[1]] = (
                    piece.astype(jnp.bfloat16)
                )


def half_transform(place, ids, gots, coeffs, owners, owned, width, occ):
    lanes = gots[0].shape[-1]
    aux = lanes // width
    occ_count = coeffs.shape[1]
    assert coeffs.shape[2] == lanes == 2 * width
    shape = jax.ShapeDtypeStruct((aux * occ_count // occ, owned * width), jnp.bfloat16)
    smem = pl.BlockSpec(memory_space=pltpu.SMEM)
    vmem = pl.BlockSpec(memory_space=pltpu.VMEM)
    shapes = [shape] * occ
    scratch = [pltpu.VMEM((owned + 1, occ_count, lanes), jnp.float32)]
    if ids is None:
        shapes.append(jax.ShapeDtypeStruct((owners, lanes), jnp.int32))
        scratch += [pltpu.SMEM((owners, lanes), jnp.int32), pltpu.SemaphoreType.DMA]
    result = pl.pallas_call(
        functools.partial(half_kernel, owned, width, owners),
        out_shape=shapes,
        in_specs=[smem] + ([] if ids is None else [smem]) + [vmem] * (1 + len(gots)),
        out_specs=[vmem] * len(shapes),
        scratch_shapes=scratch,
        cost_estimate=pl.CostEstimate(
            flops=2 * owners * LIVE * width * lanes * occ_count,
            bytes_accessed=2 * (len(gots) * gots[0].size + coeffs.size + occ * shape.size),
            transcendentals=0,
        ),
        compiler_params=pltpu.CompilerParams(vmem_limit_bytes=GRANT),
        name="half_transform",
    )(place, *([] if ids is None else [ids]), coeffs, *gots)
    return result[:occ], result[occ] if ids is None else ids


def place_kernel(layout, aux, me_ref, *refs):
    in_refs, (out_ref, wide) = refs[:-2], refs[-2:]
    slab, all_aux, _ = out_ref.shape
    chunks = 1 + max(c for parts in layout for c, _ in parts)
    for in_ref, parts in zip(in_refs, layout):
        for i, (c, j) in enumerate(parts):
            for q in range(aux):
                at = (me_ref[0] ^ j) * (chunks * aux) + c * aux + q
                row = (i * aux + q) * slab
                for t in range(wide.shape[0]):
                    wide[t, pl.ds(at, slab, stride=all_aux), :] = in_ref[
                        row : row + slab, t * 128 : (t + 1) * 128
                    ]
    for t in range(wide.shape[0]):
        out_ref[:, :, t * 128 : (t + 1) * 128] = (
            wide[t].reshape(slab, all_aux, 128).astype(out_ref.dtype)
        )


def place(me, sums, layout, slab):
    columns = sums[0].shape[1]
    rows = sum(total.shape[0] for total in sums)
    aux = sums[0].shape[0] // len(layout[0]) // slab
    vmem = pl.BlockSpec(memory_space=pltpu.VMEM)
    return pl.pallas_call(
        functools.partial(place_kernel, layout, aux),
        out_shape=jax.ShapeDtypeStruct((slab, rows // slab, columns), jnp.bfloat16),
        in_specs=[pl.BlockSpec(memory_space=pltpu.SMEM)] + [vmem] * len(sums),
        out_specs=vmem,
        scratch_shapes=[pltpu.VMEM((columns // 128, rows, 128), jnp.float32)],
        compiler_params=pltpu.CompilerParams(vmem_limit_bytes=GRANT),
        name="place",
    )(me, *sums)


def piece_layout(chunks, occ):
    near = min(2, occ)
    layout = [[(0, j) for j in range(near)]]
    for c in range(chunks):
        parts = [(c, j) for j in range(near, occ)]
        if c + 1 < chunks:
            parts += [(c + 1, j) for j in range(near)]
        if parts:
            layout.append(parts)
    return layout


def on_device(integrals, occ_coeffs, virt_coeffs, block_ids, live_mask):
    blocks = integrals[0]
    width = blocks.shape[1]
    occ_count = occ_coeffs.shape[1]
    owners = lax.axis_size("pair")
    occ = lax.axis_size("occ")
    owned = occ_coeffs.shape[0] // width // owners
    slab = occ_count // occ
    outer = owners // 2
    rows = owned * width
    me = lax.axis_index("occ").astype(jnp.int32)
    here = lax.axis_index("pair")

    def across(array, j):
        if j == 0:
            return array
        return lax.ppermute(array, "occ", [(o, o ^ j) for o in range(occ)])

    def along(array):
        return lax.ppermute(
            array, "pair", [(p, (p // 2 + 1) % outer * 2 + p % 2) for p in range(owners)]
        )

    def swap(array):
        return lax.ppermute(array, "pair", [(p, p ^ 1) for p in range(owners)])

    def gather(piece, last):
        own, other = [piece], [swap(piece)]
        for shift in range(1, outer):
            own.append(along(own[-1]))
            if last and shift == outer - 1:
                other.append(along(other[-1]))
            else:
                other.append(swap(own[-1]))
        return own, other

    def second_half(own, other):
        total = None
        for shift in range(outer):
            for flip, array in enumerate((own[shift], other[shift])):
                source = (here // 2 - shift) % outer * 2 + (here % 2 ^ flip)
                part = lax.dynamic_slice_in_dim(virt_coeffs, source * rows, rows, axis=0)
                term = jnp.dot(array, part, preferred_element_type=jnp.float32)
                total = term if total is None else total + term
        return total

    sends = pack(here.astype(jnp.int32).reshape(1), block_ids, live_mask, blocks, owners, owned)
    got = [pltpu.with_memory_space_constraint(sends[0], pltpu.HBM)]
    for n in range(1, owners):
        target = [(p, (p // 2 + n // 2) % outer * 2 + (p + n) % 2) for p in range(owners)]
        got.append(lax.ppermute(sends[n], "pair", target))
    gots = [got]
    for c, send in enumerate(sends[owners:], 1):
        gots.append([lax.all_to_all(send, "pair", split_axis=0, concat_axis=0, tiled=True)])
    spot = jnp.stack([me, here.astype(jnp.int32)])
    coeffs = occ_coeffs.reshape(-1, 2 * width, occ_count).transpose(0, 2, 1)
    parts, ids = {}, None
    for c, got in enumerate(gots):
        halves, ids = half_transform(
            spot, ids, got, coeffs, owners, owned, width, occ
        )
        for j in range(occ):
            parts[c, j] = across(halves[j], j)
    layout = piece_layout(len(gots), occ)
    results = []
    for i, names in enumerate(layout):
        piece = jnp.concatenate([parts[name] for name in names], axis=0)
        results.append(second_half(*gather(piece, i == 1)))
    return place(me.reshape(1), results, layout, slab)


def solution(mesh):
    return jax.shard_map(
        on_device,
        mesh=mesh,
        in_specs=(
            P("pair", None, None, "occ"),
            P(),
            P(None, "pair"),
            P(None, "pair", None),
            P("pair", None),
        ),
        out_specs=P("occ", None, "pair"),
        check_vma=False,
    )
```

```python
import functools

import jax
import jax.numpy as jnp
import numpy as np
from jax import lax
from jax.experimental import pallas as pl
from jax.experimental.pallas import tpu as pltpu
from jax.sharding import PartitionSpec as P


LIVE = 4
TAIL = 16
GRANT = 16 * 2**20


def relative(here, n, owners, sign=1):
    outer = owners // 2
    return lax.rem(here // 2 + sign * (n // 2) + outer, outer) * 2 + lax.rem(here + n, 2)


def pack_kernel(owned, here_ref, ids_ref, live_ref, blocks_ref, *refs):
    out_refs = refs[:-2]
    pick_ref, sems = refs[-2:]
    owners = pick_ref.shape[0]
    lanes = out_refs[0].shape[1]
    width = blocks_ref.shape[1]
    group = live_ref.shape[1] // owners
    row = lax.broadcasted_iota(jnp.int32, (TAIL, 128), 0)
    lane = lax.broadcasted_iota(jnp.int32, (TAIL, 128), 1)

    def copies(n, k, slot):
        owner = relative(here_ref[0], n, owners)
        for c in range(1 + len(out_refs) - owners):
            out = out_refs[owners + c - 1].at[owner] if c else out_refs[n]
            yield pltpu.make_async_copy(
                blocks_ref.at[slot, :, pl.ds(c * lanes, lanes)],
                out.at[pl.ds(k * width, width), :],
                sems.at[n, k, c],
            )

    for n in range(owners):
        base = relative(here_ref[0], n, owners) * group
        count = jnp.int32(0)
        for j in range(group):
            pick_ref[n, jnp.minimum(count, LIVE)] = base + j
            count = count + live_ref[0, base + j]
        tile = jnp.zeros((TAIL, 128), jnp.int32)
        for k in range(LIVE):
            slot = jnp.where(k < count, pick_ref[n, k], base)
            for copy in copies(n, k, slot):
                copy.start()
            mu = ids_ref[0, 0, slot]
            nu = jnp.where(k < count, lax.rem(ids_ref[1, 0, slot], owned), owned)
            tile = jnp.where((row == 0) & (lane == k), mu, tile)
            tile = jnp.where((row == 0) & (lane == LIVE + k), nu, tile)
        out_refs[n][LIVE * width :, :] = tile.astype(jnp.float32).astype(jnp.bfloat16)
    for n in range(owners):
        for k in range(LIVE):
            for copy in copies(n, k, 0):
                copy.wait()


def pack(here, block_ids, live_mask, blocks, owners, owned):
    _, width, minor = blocks.shape
    chunks = minor // 128
    shapes = [jax.ShapeDtypeStruct((LIVE * width + TAIL, 128), jnp.bfloat16)] * owners
    shapes += [jax.ShapeDtypeStruct((owners, LIVE * width, 128), jnp.bfloat16)] * (chunks - 1)
    smem = pl.BlockSpec(memory_space=pltpu.SMEM)
    return pl.pallas_call(
        functools.partial(pack_kernel, owned),
        out_shape=shapes,
        in_specs=[smem, smem, smem, pl.BlockSpec(memory_space=pl.ANY)],
        out_specs=[pl.BlockSpec(memory_space=pltpu.VMEM)] * len(shapes),
        scratch_shapes=[
            pltpu.SMEM((owners, LIVE + 1), jnp.int32),
            pltpu.SemaphoreType.DMA((owners, LIVE, chunks)),
        ],
        name="pack_live",
    )(here, block_ids, live_mask, pltpu.with_memory_space_constraint(blocks, pltpu.HBM))


def half_kernel(owned, width, owners, place_ref, *refs):
    refs = list(refs)
    given = refs.pop(0) if refs[0].dtype == jnp.int32 else None
    coeff_ref = refs.pop(0)
    if given is None:
        got_refs, refs = refs[:owners], refs[owners:]
        total, ids_smem, sem = refs[-3:]
        out_refs, ids_vmem = refs[:-4], refs[-4]
        for n, got_ref in enumerate(got_refs):
            ids_vmem[n : n + 1, :] = (
                got_ref[LIVE * width :, :][0:1].astype(jnp.float32).astype(jnp.int32)
            )
        ids = pltpu.make_async_copy(ids_vmem, ids_smem, sem)
        ids.start()
        total[...] = jnp.zeros_like(total)
        ids.wait()
    else:
        got_ref, ids_smem, out_refs, total = refs[0], given, refs[1:-1], refs[-1]
        got_refs = [got_ref.at[relative(place_ref[1], n, owners, -1)] for n in range(owners)]
        total[...] = jnp.zeros_like(total)
    aux = got_refs[0].shape[1] // width
    low = lax.broadcasted_iota(jnp.int32, (width, 2 * width), 1) < width
    high = lax.broadcasted_iota(jnp.int32, (total.shape[1], 2 * width), 1) // width
    for n, got_ref in enumerate(got_refs):
        for k in range(LIVE):
            mu = ids_smem[n, k]
            nu = ids_smem[n, LIVE + k]
            block = got_ref[k * width : (k + 1) * width, :]
            turned = pltpu.roll(block.astype(jnp.float32), width, 1).astype(block.dtype)
            stacked = jnp.concatenate(
                [jnp.where(low, block, turned), jnp.where(low, turned, block)], axis=0
            )
            coeff = coeff_ref[mu // 2]
            coeff = jnp.where((high ^ lax.rem(mu, 2)) == 0, coeff, jnp.zeros_like(coeff))
            total[nu] += lax.dot_general(
                coeff, stacked, (((1,), (1,)), ((), ())), preferred_element_type=jnp.float32
            )

    slab = total.shape[1] // len(out_refs)
    for j, out_ref in enumerate(out_refs):
        start = pl.multiple_of((place_ref[0] ^ j) * slab, slab)
        for b in range(0, owned, 2):
            pair = [total[c, pl.ds(start, slab), :] for c in range(b, min(b + 2, owned))]
            for q in range(aux):
                cut = [t[:, q * width : (q + 1) * width] for t in pair]
                piece = cut[0] if len(cut) == 1 else jnp.concatenate(cut, axis=1)
                out_ref[q * slab : (q + 1) * slab, b * width : b * width + piece.shape[1]] = (
                    piece.astype(jnp.bfloat16)
                )


def half_transform(place, ids, gots, coeffs, owners, owned, width, occ):
    lanes = gots[0].shape[-1]
    aux = lanes // width
    occ_count = coeffs.shape[1]
    assert coeffs.shape[2] == lanes == 2 * width
    shape = jax.ShapeDtypeStruct((aux * occ_count // occ, owned * width), jnp.bfloat16)
    smem = pl.BlockSpec(memory_space=pltpu.SMEM)
    vmem = pl.BlockSpec(memory_space=pltpu.VMEM)
    shapes = [shape] * occ
    scratch = [pltpu.VMEM((owned + 1, occ_count, lanes), jnp.float32)]
    if ids is None:
        shapes.append(jax.ShapeDtypeStruct((owners, lanes), jnp.int32))
        scratch += [pltpu.SMEM((owners, lanes), jnp.int32), pltpu.SemaphoreType.DMA]
    result = pl.pallas_call(
        functools.partial(half_kernel, owned, width, owners),
        out_shape=shapes,
        in_specs=[smem] + ([] if ids is None else [smem]) + [vmem] * (1 + len(gots)),
        out_specs=[vmem] * len(shapes),
        scratch_shapes=scratch,
        cost_estimate=pl.CostEstimate(
            flops=2 * owners * LIVE * width * lanes * occ_count,
            bytes_accessed=2 * (len(gots) * gots[0].size + coeffs.size + occ * shape.size),
            transcendentals=0,
        ),
        compiler_params=pltpu.CompilerParams(vmem_limit_bytes=GRANT),
        name="half_transform",
    )(place, *([] if ids is None else [ids]), coeffs, *gots)
    return result[:occ], result[occ] if ids is None else ids


def place_kernel(order_ref, *refs):
    in_refs, (out_ref, rounded) = refs[:-2], refs[-2:]
    row = 0
    for in_ref in in_refs:
        rounded[row : row + in_ref.shape[0], :] = in_ref[...].astype(rounded.dtype)
        row += in_ref.shape[0]
    placed = jnp.dot(order_ref[...], rounded[...], preferred_element_type=jnp.float32)
    out_ref[...] = placed.astype(out_ref.dtype).reshape(out_ref.shape)


def place(order, sums, slab):
    columns = sums[0].shape[1]
    rows = order.shape[0]
    vmem = pl.BlockSpec(memory_space=pltpu.VMEM)
    return pl.pallas_call(
        place_kernel,
        out_shape=jax.ShapeDtypeStruct((slab, rows // slab, columns), jnp.bfloat16),
        in_specs=[vmem] * (1 + len(sums)),
        out_specs=vmem,
        scratch_shapes=[pltpu.VMEM((rows, columns), jnp.bfloat16)],
        compiler_params=pltpu.CompilerParams(vmem_limit_bytes=GRANT),
        name="place",
    )(order, *sums)


def target_rows(me, layout, occ, chunks, aux, slab):
    names = [(c, j, q, i) for parts in layout for c, j in parts for q in range(aux) for i in range(slab)]
    c, j, q, i = (np.array(column, np.int32) for column in zip(*names))
    return (i * (occ * chunks * aux) + (j ^ me) * (chunks * aux) + c * aux + q).reshape(1, -1)


def stage_kernel(in_ref, target_ref, out_ref, order_ref, sems):
    rows = out_ref.shape[0] // sems.shape[0]
    copies = [
        pltpu.make_async_copy(
            in_ref.at[pl.ds(i * rows, rows), :], out_ref.at[pl.ds(i * rows, rows), :], sems.at[i]
        )
        for i in range(sems.shape[0])
    ]
    for copy in copies:
        copy.start()
    row = lax.broadcasted_iota(jnp.int32, order_ref.shape, 0)
    order_ref[...] = (row == target_ref[...]).astype(jnp.float32).astype(order_ref.dtype)
    for copy in copies:
        copy.wait()


def stage(array, target, pieces):
    vmem = pl.BlockSpec(memory_space=pltpu.VMEM)
    size = target.shape[1]
    return pl.pallas_call(
        stage_kernel,
        out_shape=[
            jax.ShapeDtypeStruct(array.shape, array.dtype),
            jax.ShapeDtypeStruct((size, size), jnp.bfloat16),
        ],
        in_specs=[pl.BlockSpec(memory_space=pl.ANY), vmem],
        out_specs=[vmem] * 2,
        scratch_shapes=[pltpu.SemaphoreType.DMA((pieces,))],
        compiler_params=pltpu.CompilerParams(vmem_limit_bytes=GRANT),
        name="stage",
    )(pltpu.with_memory_space_constraint(array, pltpu.HBM), target)


def piece_layout(chunks, occ):
    near = min(2, occ)
    layout = [[(0, j) for j in range(near)]]
    for c in range(chunks):
        parts = [(c, j) for j in range(near, occ)]
        if c + 1 < chunks:
            parts = [(c + 1, j) for j in range(near)] + parts
        if parts:
            layout.append(parts)
    return layout


def on_device(integrals, occ_coeffs, virt_coeffs, block_ids, live_mask):
    blocks = integrals[0]
    width = blocks.shape[1]
    occ_count = occ_coeffs.shape[1]
    owners = lax.axis_size("pair")
    occ = lax.axis_size("occ")
    owned = occ_coeffs.shape[0] // width // owners
    slab = occ_count // occ
    outer = owners // 2
    rows = owned * width
    me = lax.axis_index("occ").astype(jnp.int32)
    here = lax.axis_index("pair")

    def across(array, j):
        if j == 0:
            return array
        return lax.ppermute(array, "occ", [(o, o ^ j) for o in range(occ)])

    def along(array):
        return lax.ppermute(
            array, "pair", [(p, (p // 2 + 1) % outer * 2 + p % 2) for p in range(owners)]
        )

    def swap(array):
        return lax.ppermute(array, "pair", [(p, p ^ 1) for p in range(owners)])

    def gather(piece, last):
        own, other = [piece], [swap(piece)]
        for shift in range(1, outer):
            own.append(along(own[-1]))
            if last and shift == outer - 1:
                other.append(along(other[-1]))
            else:
                other.append(swap(own[-1]))
        return own, other

    def second_half(own, other):
        total = None
        for shift in range(outer):
            for flip, array in enumerate((own[shift], other[shift])):
                source = (here // 2 - shift) % outer * 2 + (here % 2 ^ flip)
                part = lax.dynamic_slice_in_dim(virt, source * rows, rows, axis=0)
                term = jnp.dot(array, part, preferred_element_type=jnp.float32)
                total = term if total is None else total + term
        return total

    sends = pack(here.astype(jnp.int32).reshape(1), block_ids, live_mask, blocks, owners, owned)
    got = [pltpu.with_memory_space_constraint(sends[0], pltpu.HBM)]
    for n in range(1, owners):
        target = [(p, (p // 2 + n // 2) % outer * 2 + (p + n) % 2) for p in range(owners)]
        got.append(lax.ppermute(sends[n], "pair", target))
    gots = [got]
    for c, send in enumerate(sends[owners:], 1):
        gots.append([lax.all_to_all(send, "pair", split_axis=0, concat_axis=0, tiled=True)])
    spot = jnp.stack([me, here.astype(jnp.int32)])
    coeffs = occ_coeffs.reshape(-1, 2 * width, occ_count).transpose(0, 2, 1)
    parts, ids = {}, None
    for c, got in enumerate(gots):
        halves, ids = half_transform(
            spot, ids, got, coeffs, owners, owned, width, occ
        )
        for j in range(occ):
            parts[c, j] = across(halves[j], j)
    layout = piece_layout(len(gots), occ)
    target = target_rows(me, layout, occ, len(gots), 2, slab)
    virt, row_order = stage(virt_coeffs, target, 8)
    results = []
    for i, names in enumerate(layout):
        piece = jnp.concatenate([parts[name] for name in names], axis=0)
        results.append(second_half(*gather(piece, i == 1)))
    return place(row_order, results, slab)


def solution(mesh):
    return jax.shard_map(
        on_device,
        mesh=mesh,
        in_specs=(
            P("pair", None, None, "occ"),
            P(),
            P(None, "pair"),
            P(None, "pair", None),
            P("pair", None),
        ),
        out_specs=P("occ", None, "pair"),
        check_vma=False,
    )
```

```python
import functools

import jax
import jax.numpy as jnp
from jax import lax
from jax.experimental import pallas as pl
from jax.experimental.pallas import tpu as pltpu
from jax.sharding import PartitionSpec as P


LIVE = 4
TAIL = 8
GRANT = 16 * 2**20


def relative(here, n, owners, sign=1):
    outer = owners // 2
    return lax.rem(here // 2 + sign * (n // 2) + outer, outer) * 2 + lax.rem(here + n, 2)


def pack_kernel(owned, here_ref, ids_ref, live_ref, blocks_ref, *refs):
    out_refs = refs[:-2]
    pick_ref, sems = refs[-2:]
    owners = pick_ref.shape[0]
    lanes = out_refs[0].shape[1]
    width = blocks_ref.shape[1]
    group = live_ref.shape[1] // owners
    row = lax.broadcasted_iota(jnp.int32, (TAIL, 128), 0)
    lane = lax.broadcasted_iota(jnp.int32, (TAIL, 128), 1)

    def copies(n, k, slot):
        owner = relative(here_ref[0], n, owners)
        for c in range(1 + len(out_refs) - owners):
            out = out_refs[owners + c - 1].at[owner] if c else out_refs[n]
            yield pltpu.make_async_copy(
                blocks_ref.at[slot, :, pl.ds(c * lanes, lanes)],
                out.at[pl.ds(k * width, width), :],
                sems.at[n, k, c],
            )

    for n in range(owners):
        base = relative(here_ref[0], n, owners) * group
        count = jnp.int32(0)
        for j in range(group):
            pick_ref[n, jnp.minimum(count, LIVE)] = base + j
            count = count + live_ref[0, base + j]
        tile = jnp.zeros((TAIL, 128), jnp.int32)
        for k in range(LIVE):
            slot = jnp.where(k < count, pick_ref[n, k], base)
            for copy in copies(n, k, slot):
                copy.start()
            mu = ids_ref[0, 0, slot]
            nu = jnp.where(k < count, lax.rem(ids_ref[1, 0, slot], owned), owned)
            tile = jnp.where((row == 0) & (lane == k), mu, tile)
            tile = jnp.where((row == 0) & (lane == LIVE + k), nu, tile)
        out_refs[n][LIVE * width :, :] = tile.astype(jnp.float32).astype(jnp.bfloat16)
    for n in range(owners):
        for k in range(LIVE):
            for copy in copies(n, k, 0):
                copy.wait()


def pack(here, block_ids, live_mask, blocks, owners, owned):
    _, width, minor = blocks.shape
    chunks = minor // 128
    shapes = [jax.ShapeDtypeStruct((LIVE * width + TAIL, 128), jnp.bfloat16)] * owners
    shapes += [jax.ShapeDtypeStruct((owners, LIVE * width, 128), jnp.bfloat16)] * (chunks - 1)
    smem = pl.BlockSpec(memory_space=pltpu.SMEM)
    return pl.pallas_call(
        functools.partial(pack_kernel, owned),
        out_shape=shapes,
        in_specs=[smem, smem, smem, pl.BlockSpec(memory_space=pl.ANY)],
        out_specs=[pl.BlockSpec(memory_space=pltpu.VMEM)] * len(shapes),
        scratch_shapes=[
            pltpu.SMEM((owners, LIVE + 1), jnp.int32),
            pltpu.SemaphoreType.DMA((owners, LIVE, chunks)),
        ],
        name="pack_live",
    )(here, block_ids, live_mask, pltpu.with_memory_space_constraint(blocks, pltpu.HBM))


def half_kernel(owned, width, owners, place_ref, *refs):
    refs = list(refs)
    given = refs.pop(0) if refs[0].dtype == jnp.int32 else None
    coeff_ref = refs.pop(0)
    if given is None:
        got_refs, refs = refs[:owners], refs[owners:]
        total, ids_smem, sem = refs[-3:]
        out_refs, ids_vmem = refs[:-4], refs[-4]
        for n, got_ref in enumerate(got_refs):
            ids_vmem[n : n + 1, :] = (
                got_ref[LIVE * width :, :][0:1].astype(jnp.float32).astype(jnp.int32)
            )
        ids = pltpu.make_async_copy(ids_vmem, ids_smem, sem)
        ids.start()
        total[...] = jnp.zeros_like(total)
        ids.wait()
    else:
        got_ref, ids_smem, out_refs, total = refs[0], given, refs[1:-1], refs[-1]
        got_refs = [got_ref.at[relative(place_ref[1], n, owners, -1)] for n in range(owners)]
        total[...] = jnp.zeros_like(total)
    aux = got_refs[0].shape[1] // width
    low = lax.broadcasted_iota(jnp.int32, (width, 2 * width), 1) < width
    high = lax.broadcasted_iota(jnp.int32, (total.shape[1], 2 * width), 1) // width
    for n, got_ref in enumerate(got_refs):
        for k in range(LIVE):
            mu = ids_smem[n, k]
            nu = ids_smem[n, LIVE + k]
            block = got_ref[k * width : (k + 1) * width, :]
            turned = pltpu.roll(block.astype(jnp.float32), width, 1).astype(block.dtype)
            stacked = jnp.concatenate(
                [jnp.where(low, block, turned), jnp.where(low, turned, block)], axis=0
            )
            coeff = coeff_ref[mu // 2]
            coeff = jnp.where((high ^ lax.rem(mu, 2)) == 0, coeff, jnp.zeros_like(coeff))
            total[nu] += lax.dot_general(
                coeff, stacked, (((1,), (1,)), ((), ())), preferred_element_type=jnp.float32
            )

    slab = total.shape[1] // len(out_refs)
    for j, out_ref in enumerate(out_refs):
        start = pl.multiple_of((place_ref[0] ^ j) * slab, slab)
        for b in range(0, owned, 2):
            pair = [total[c, pl.ds(start, slab), :] for c in range(b, min(b + 2, owned))]
            for q in range(aux):
                cut = [t[:, q * width : (q + 1) * width] for t in pair]
                piece = cut[0] if len(cut) == 1 else jnp.concatenate(cut, axis=1)
                out_ref[q * slab : (q + 1) * slab, b * width : b * width + piece.shape[1]] = (
                    piece.astype(jnp.bfloat16)
                )


def half_transform(place, ids, gots, coeffs, owners, owned, width, occ):
    lanes = gots[0].shape[-1]
    aux = lanes // width
    occ_count = coeffs.shape[1]
    assert coeffs.shape[2] == lanes == 2 * width
    shape = jax.ShapeDtypeStruct((aux * occ_count // occ, owned * width), jnp.bfloat16)
    smem = pl.BlockSpec(memory_space=pltpu.SMEM)
    vmem = pl.BlockSpec(memory_space=pltpu.VMEM)
    shapes = [shape] * occ
    scratch = [pltpu.VMEM((owned + 1, occ_count, lanes), jnp.float32)]
    if ids is None:
        shapes.append(jax.ShapeDtypeStruct((owners, lanes), jnp.int32))
        scratch += [pltpu.SMEM((owners, lanes), jnp.int32), pltpu.SemaphoreType.DMA]
    result = pl.pallas_call(
        functools.partial(half_kernel, owned, width, owners),
        out_shape=shapes,
        in_specs=[smem] + ([] if ids is None else [smem]) + [vmem] * (1 + len(gots)),
        out_specs=[vmem] * len(shapes),
        scratch_shapes=scratch,
        cost_estimate=pl.CostEstimate(
            flops=2 * owners * LIVE * width * lanes * occ_count,
            bytes_accessed=2 * (len(gots) * gots[0].size + coeffs.size + occ * shape.size),
            transcendentals=0,
        ),
        compiler_params=pltpu.CompilerParams(vmem_limit_bytes=GRANT),
        name="half_transform",
    )(place, *([] if ids is None else [ids]), coeffs, *gots)
    return result[:occ], result[occ] if ids is None else ids


def place_kernel(layout, aux, me_ref, *refs):
    in_refs, (out_ref, wide) = refs[:-2], refs[-2:]
    slab, all_aux, _ = out_ref.shape
    chunks = 1 + max(c for parts in layout for c, _ in parts)
    for in_ref, parts in zip(in_refs, layout):
        for i, (c, j) in enumerate(parts):
            for q in range(aux):
                at = (me_ref[0] ^ j) * (chunks * aux) + c * aux + q
                row = (i * aux + q) * slab
                for t in range(wide.shape[0]):
                    wide[t, pl.ds(at, slab, stride=all_aux), :] = in_ref[
                        row : row + slab, t * 128 : (t + 1) * 128
                    ]
    for t in range(wide.shape[0]):
        out_ref[:, :, t * 128 : (t + 1) * 128] = (
            wide[t].reshape(slab, all_aux, 128).astype(out_ref.dtype)
        )


def place(me, sums, layout, slab):
    columns = sums[0].shape[1]
    rows = sum(total.shape[0] for total in sums)
    aux = sums[0].shape[0] // len(layout[0]) // slab
    vmem = pl.BlockSpec(memory_space=pltpu.VMEM)
    return pl.pallas_call(
        functools.partial(place_kernel, layout, aux),
        out_shape=jax.ShapeDtypeStruct((slab, rows // slab, columns), jnp.bfloat16),
        in_specs=[pl.BlockSpec(memory_space=pltpu.SMEM)] + [vmem] * len(sums),
        out_specs=vmem,
        scratch_shapes=[pltpu.VMEM((columns // 128, rows, 128), jnp.float32)],
        compiler_params=pltpu.CompilerParams(vmem_limit_bytes=GRANT),
        name="place",
    )(me, *sums)


def stage_kernel(in_ref, out_ref, sems):
    rows = out_ref.shape[0] // sems.shape[0]
    copies = [
        pltpu.make_async_copy(
            in_ref.at[pl.ds(i * rows, rows), :], out_ref.at[pl.ds(i * rows, rows), :], sems.at[i]
        )
        for i in range(sems.shape[0])
    ]
    for copy in copies:
        copy.start()
    for copy in copies:
        copy.wait()


def stage(array, pieces):
    return pl.pallas_call(
        stage_kernel,
        out_shape=jax.ShapeDtypeStruct(array.shape, array.dtype),
        in_specs=[pl.BlockSpec(memory_space=pl.ANY)],
        out_specs=pl.BlockSpec(memory_space=pltpu.VMEM),
        scratch_shapes=[pltpu.SemaphoreType.DMA((pieces,))],
        compiler_params=pltpu.CompilerParams(vmem_limit_bytes=GRANT),
        name="stage",
    )(pltpu.with_memory_space_constraint(array, pltpu.HBM))


def piece_layout(chunks, occ):
    near = min(2, occ)
    layout = [[(0, j) for j in range(near)]]
    for c in range(chunks):
        parts = [(c, j) for j in range(near, occ)]
        if c + 1 < chunks:
            parts = [(c + 1, j) for j in range(near)] + parts
        if parts:
            layout.append(parts)
    return layout


def on_device(integrals, occ_coeffs, virt_coeffs, block_ids, live_mask):
    blocks = integrals[0]
    width = blocks.shape[1]
    occ_count = occ_coeffs.shape[1]
    owners = lax.axis_size("pair")
    occ = lax.axis_size("occ")
    owned = occ_coeffs.shape[0] // width // owners
    slab = occ_count // occ
    outer = owners // 2
    rows = owned * width
    me = lax.axis_index("occ").astype(jnp.int32)
    here = lax.axis_index("pair")

    def across(array, j):
        if j == 0:
            return array
        return lax.ppermute(array, "occ", [(o, o ^ j) for o in range(occ)])

    def along(array):
        return lax.ppermute(
            array, "pair", [(p, (p // 2 + 1) % outer * 2 + p % 2) for p in range(owners)]
        )

    def swap(array):
        return lax.ppermute(array, "pair", [(p, p ^ 1) for p in range(owners)])

    def gather(piece, last):
        own, other = [piece], [swap(piece)]
        for shift in range(1, outer):
            own.append(along(own[-1]))
            if last and shift == outer - 1:
                other.append(along(other[-1]))
            else:
                other.append(swap(own[-1]))
        return own, other

    def second_half(own, other):
        total = None
        for shift in range(outer):
            for flip, array in enumerate((own[shift], other[shift])):
                source = (here // 2 - shift) % outer * 2 + (here % 2 ^ flip)
                part = lax.dynamic_slice_in_dim(virt, source * rows, rows, axis=0)
                term = jnp.dot(array, part, preferred_element_type=jnp.float32)
                total = term if total is None else total + term
        return total

    sends = pack(here.astype(jnp.int32).reshape(1), block_ids, live_mask, blocks, owners, owned)
    got = [pltpu.with_memory_space_constraint(sends[0], pltpu.HBM)]
    for n in range(1, owners):
        target = [(p, (p // 2 + n // 2) % outer * 2 + (p + n) % 2) for p in range(owners)]
        got.append(lax.ppermute(sends[n], "pair", target))
    gots = [got]
    for c, send in enumerate(sends[owners:], 1):
        gots.append([lax.all_to_all(send, "pair", split_axis=0, concat_axis=0, tiled=True)])
    spot = jnp.stack([me, here.astype(jnp.int32)])
    coeffs = occ_coeffs.reshape(-1, 2 * width, occ_count).transpose(0, 2, 1)
    parts, ids = {}, None
    for c, got in enumerate(gots):
        halves, ids = half_transform(
            spot, ids, got, coeffs, owners, owned, width, occ
        )
        for j in range(occ):
            parts[c, j] = across(halves[j], j)
    layout = piece_layout(len(gots), occ)
    virt = stage(virt_coeffs, 8)
    results = []
    for i, names in enumerate(layout):
        piece = jnp.concatenate([parts[name] for name in names], axis=0)
        results.append(second_half(*gather(piece, i == 1)))
    return place(me.reshape(1), results, layout, slab)


def solution(mesh):
    return jax.shard_map(
        on_device,
        mesh=mesh,
        in_specs=(
            P("pair", None, None, "occ"),
            P(),
            P(None, "pair"),
            P(None, "pair", None),
            P("pair", None),
        ),
        out_specs=P("occ", None, "pair"),
        check_vma=False,
    )
```

```python
import functools

import jax
import jax.numpy as jnp
from jax import lax
from jax.experimental import pallas as pl
from jax.experimental.pallas import tpu as pltpu
from jax.sharding import PartitionSpec as P


LIVE = 4
TAIL = 16
GRANT = 16 * 2**20


def relative(here, n, owners, sign=1):
    outer = owners // 2
    return lax.rem(here // 2 + sign * (n // 2) + outer, outer) * 2 + lax.rem(here + n, 2)


def pack_kernel(owned, here_ref, ids_ref, live_ref, blocks_ref, *refs):
    out_refs = refs[:-2]
    pick_ref, sems = refs[-2:]
    owners = pick_ref.shape[0]
    lanes = out_refs[0].shape[1]
    width = blocks_ref.shape[1]
    group = live_ref.shape[1] // owners
    row = lax.broadcasted_iota(jnp.int32, (TAIL, 128), 0)
    lane = lax.broadcasted_iota(jnp.int32, (TAIL, 128), 1)

    def copies(n, k, slot):
        owner = relative(here_ref[0], n, owners)
        for c in range(1 + len(out_refs) - owners):
            out = out_refs[owners + c - 1].at[owner] if c else out_refs[n]
            yield pltpu.make_async_copy(
                blocks_ref.at[slot, :, pl.ds(c * lanes, lanes)],
                out.at[pl.ds(k * width, width), :],
                sems.at[n, k, c],
            )

    for n in range(owners):
        base = relative(here_ref[0], n, owners) * group
        count = jnp.int32(0)
        for j in range(group):
            pick_ref[n, jnp.minimum(count, LIVE)] = base + j
            count = count + live_ref[0, base + j]
        tile = jnp.zeros((TAIL, 128), jnp.int32)
        for k in range(LIVE):
            slot = jnp.where(k < count, pick_ref[n, k], base)
            for copy in copies(n, k, slot):
                copy.start()
            mu = ids_ref[0, 0, slot]
            nu = jnp.where(k < count, lax.rem(ids_ref[1, 0, slot], owned), owned)
            tile = jnp.where((row == 0) & (lane == k), mu, tile)
            tile = jnp.where((row == 0) & (lane == LIVE + k), nu, tile)
        out_refs[n][LIVE * width :, :] = tile.astype(jnp.float32).astype(jnp.bfloat16)
    for n in range(owners):
        for k in range(LIVE):
            for copy in copies(n, k, 0):
                copy.wait()


def pack(here, block_ids, live_mask, blocks, owners, owned):
    _, width, minor = blocks.shape
    chunks = minor // 128
    shapes = [jax.ShapeDtypeStruct((LIVE * width + TAIL, 128), jnp.bfloat16)] * owners
    shapes += [jax.ShapeDtypeStruct((owners, LIVE * width, 128), jnp.bfloat16)] * (chunks - 1)
    smem = pl.BlockSpec(memory_space=pltpu.SMEM)
    return pl.pallas_call(
        functools.partial(pack_kernel, owned),
        out_shape=shapes,
        in_specs=[smem, smem, smem, pl.BlockSpec(memory_space=pl.ANY)],
        out_specs=[pl.BlockSpec(memory_space=pltpu.VMEM)] * len(shapes),
        scratch_shapes=[
            pltpu.SMEM((owners, LIVE + 1), jnp.int32),
            pltpu.SemaphoreType.DMA((owners, LIVE, chunks)),
        ],
        name="pack_live",
    )(here, block_ids, live_mask, pltpu.with_memory_space_constraint(blocks, pltpu.HBM))


def half_kernel(owned, width, owners, place_ref, *refs):
    refs = list(refs)
    given = refs.pop(0) if refs[0].dtype == jnp.int32 else None
    coeff_ref = refs.pop(0)
    if given is None:
        got_refs, refs = refs[:owners], refs[owners:]
        total, ids_smem, sem = refs[-3:]
        out_refs, ids_vmem = refs[:-4], refs[-4]
        for n, got_ref in enumerate(got_refs):
            ids_vmem[n : n + 1, :] = (
                got_ref[LIVE * width :, :][0:1].astype(jnp.float32).astype(jnp.int32)
            )
        ids = pltpu.make_async_copy(ids_vmem, ids_smem, sem)
        ids.start()
        total[...] = jnp.zeros_like(total)
        ids.wait()
    else:
        got_ref, ids_smem, out_refs, total = refs[0], given, refs[1:-1], refs[-1]
        got_refs = [got_ref.at[relative(place_ref[1], n, owners, -1)] for n in range(owners)]
        total[...] = jnp.zeros_like(total)
    aux = got_refs[0].shape[1] // width
    low = lax.broadcasted_iota(jnp.int32, (width, 2 * width), 1) < width
    high = lax.broadcasted_iota(jnp.int32, (total.shape[1], 2 * width), 1) // width
    for n, got_ref in enumerate(got_refs):
        for k in range(LIVE):
            mu = ids_smem[n, k]
            nu = ids_smem[n, LIVE + k]
            block = got_ref[k * width : (k + 1) * width, :]
            turned = pltpu.roll(block.astype(jnp.float32), width, 1).astype(block.dtype)
            stacked = jnp.concatenate(
                [jnp.where(low, block, turned), jnp.where(low, turned, block)], axis=0
            )
            coeff = coeff_ref[mu // 2]
            coeff = jnp.where((high ^ lax.rem(mu, 2)) == 0, coeff, jnp.zeros_like(coeff))
            total[nu] += lax.dot_general(
                coeff, stacked, (((1,), (1,)), ((), ())), preferred_element_type=jnp.float32
            )

    slab = total.shape[1] // len(out_refs)
    for j, out_ref in enumerate(out_refs):
        start = pl.multiple_of((place_ref[0] ^ j) * slab, slab)
        for b in range(0, owned, 2):
            pair = [total[c, pl.ds(start, slab), :] for c in range(b, min(b + 2, owned))]
            for q in range(aux):
                cut = [t[:, q * width : (q + 1) * width] for t in pair]
                piece = cut[0] if len(cut) == 1 else jnp.concatenate(cut, axis=1)
                out_ref[q * slab : (q + 1) * slab, b * width : b * width + piece.shape[1]] = (
                    piece.astype(jnp.bfloat16)
                )


def half_transform(place, ids, gots, coeffs, owners, owned, width, occ):
    lanes = gots[0].shape[-1]
    aux = lanes // width
    occ_count = coeffs.shape[1]
    assert coeffs.shape[2] == lanes == 2 * width
    shape = jax.ShapeDtypeStruct((aux * occ_count // occ, owned * width), jnp.bfloat16)
    smem = pl.BlockSpec(memory_space=pltpu.SMEM)
    vmem = pl.BlockSpec(memory_space=pltpu.VMEM)
    shapes = [shape] * occ
    scratch = [pltpu.VMEM((owned + 1, occ_count, lanes), jnp.float32)]
    if ids is None:
        shapes.append(jax.ShapeDtypeStruct((owners, lanes), jnp.int32))
        scratch += [pltpu.SMEM((owners, lanes), jnp.int32), pltpu.SemaphoreType.DMA]
    result = pl.pallas_call(
        functools.partial(half_kernel, owned, width, owners),
        out_shape=shapes,
        in_specs=[smem] + ([] if ids is None else [smem]) + [vmem] * (1 + len(gots)),
        out_specs=[vmem] * len(shapes),
        scratch_shapes=scratch,
        cost_estimate=pl.CostEstimate(
            flops=2 * owners * LIVE * width * lanes * occ_count,
            bytes_accessed=2 * (len(gots) * gots[0].size + coeffs.size + occ * shape.size),
            transcendentals=0,
        ),
        compiler_params=pltpu.CompilerParams(vmem_limit_bytes=GRANT),
        name="half_transform",
    )(place, *([] if ids is None else [ids]), coeffs, *gots)
    return result[:occ], result[occ] if ids is None else ids


def place_kernel(layout, aux, me_ref, *refs):
    in_refs, (out_ref, wide) = refs[:-2], refs[-2:]
    slab, all_aux, _ = out_ref.shape
    chunks = 1 + max(c for parts in layout for c, _ in parts)
    for in_ref, parts in zip(in_refs, layout):
        for i, (c, j) in enumerate(parts):
            for q in range(aux):
                at = (me_ref[0] ^ j) * (chunks * aux) + c * aux + q
                row = (i * aux + q) * slab
                for t in range(wide.shape[0]):
                    wide[t, pl.ds(at, slab, stride=all_aux), :] = in_ref[
                        row : row + slab, t * 128 : (t + 1) * 128
                    ]
    for t in range(wide.shape[0]):
        out_ref[:, :, t * 128 : (t + 1) * 128] = (
            wide[t, : slab * all_aux, :].reshape(slab, all_aux, 128).astype(out_ref.dtype)
        )


def place(me, sums, layout, slab):
    columns = sums[0].shape[1]
    rows = sum(total.shape[0] for total in sums)
    aux = sums[0].shape[0] // len(layout[0]) // slab
    vmem = pl.BlockSpec(memory_space=pltpu.VMEM)
    return pl.pallas_call(
        functools.partial(place_kernel, layout, aux),
        out_shape=jax.ShapeDtypeStruct((slab, rows // slab, columns), jnp.bfloat16),
        in_specs=[pl.BlockSpec(memory_space=pltpu.SMEM)] + [vmem] * len(sums),
        out_specs=vmem,
        scratch_shapes=[pltpu.VMEM((columns // 128, rows + rows // slab, 128), jnp.float32)],
        compiler_params=pltpu.CompilerParams(vmem_limit_bytes=GRANT),
        name="place",
    )(me, *sums)


def stage_kernel(in_ref, out_ref, sems):
    rows = out_ref.shape[0] // sems.shape[0]
    copies = [
        pltpu.make_async_copy(
            in_ref.at[pl.ds(i * rows, rows), :], out_ref.at[pl.ds(i * rows, rows), :], sems.at[i]
        )
        for i in range(sems.shape[0])
    ]
    for copy in copies:
        copy.start()
    for copy in copies:
        copy.wait()


def stage(array, pieces):
    return pl.pallas_call(
        stage_kernel,
        out_shape=jax.ShapeDtypeStruct(array.shape, array.dtype),
        in_specs=[pl.BlockSpec(memory_space=pl.ANY)],
        out_specs=pl.BlockSpec(memory_space=pltpu.VMEM),
        scratch_shapes=[pltpu.SemaphoreType.DMA((pieces,))],
        compiler_params=pltpu.CompilerParams(vmem_limit_bytes=GRANT),
        name="stage",
    )(pltpu.with_memory_space_constraint(array, pltpu.HBM))


def piece_layout(chunks, occ):
    near = min(2, occ)
    layout = [[(0, j) for j in range(near)]]
    for c in range(chunks):
        parts = [(c, j) for j in range(near, occ)]
        if c + 1 < chunks:
            parts = [(c + 1, j) for j in range(near)] + parts
        if parts:
            layout.append(parts)
    return layout


def on_device(integrals, occ_coeffs, virt_coeffs, block_ids, live_mask):
    blocks = integrals[0]
    width = blocks.shape[1]
    occ_count = occ_coeffs.shape[1]
    owners = lax.axis_size("pair")
    occ = lax.axis_size("occ")
    owned = occ_coeffs.shape[0] // width // owners
    slab = occ_count // occ
    outer = owners // 2
    rows = owned * width
    me = lax.axis_index("occ").astype(jnp.int32)
    here = lax.axis_index("pair")

    def across(array, j):
        if j == 0:
            return array
        return lax.ppermute(array, "occ", [(o, o ^ j) for o in range(occ)])

    def along(array):
        return lax.ppermute(
            array, "pair", [(p, (p // 2 + 1) % outer * 2 + p % 2) for p in range(owners)]
        )

    def swap(array):
        return lax.ppermute(array, "pair", [(p, p ^ 1) for p in range(owners)])

    def gather(piece, last):
        own, other = [piece], [swap(piece)]
        for shift in range(1, outer):
            own.append(along(own[-1]))
            if last and shift == outer - 1:
                other.append(along(other[-1]))
            else:
                other.append(swap(own[-1]))
        return own, other

    def second_half(own, other):
        total = None
        for shift in range(outer):
            for flip, array in enumerate((own[shift], other[shift])):
                source = (here // 2 - shift) % outer * 2 + (here % 2 ^ flip)
                part = lax.dynamic_slice_in_dim(virt, source * rows, rows, axis=0)
                term = jnp.dot(array, part, preferred_element_type=jnp.float32)
                total = term if total is None else total + term
        return total

    sends = pack(here.astype(jnp.int32).reshape(1), block_ids, live_mask, blocks, owners, owned)
    got = [pltpu.with_memory_space_constraint(sends[0], pltpu.HBM)]
    for n in range(1, owners):
        target = [(p, (p // 2 + n // 2) % outer * 2 + (p + n) % 2) for p in range(owners)]
        got.append(lax.ppermute(sends[n], "pair", target))
    gots = [got]
    for c, send in enumerate(sends[owners:], 1):
        gots.append([lax.all_to_all(send, "pair", split_axis=0, concat_axis=0, tiled=True)])
    spot = jnp.stack([me, here.astype(jnp.int32)])
    coeffs = occ_coeffs.reshape(-1, 2 * width, occ_count).transpose(0, 2, 1)
    parts, ids = {}, None
    for c, got in enumerate(gots):
        halves, ids = half_transform(
            spot, ids, got, coeffs, owners, owned, width, occ
        )
        for j in range(occ):
            parts[c, j] = across(halves[j], j)
    layout = piece_layout(len(gots), occ)
    virt = stage(virt_coeffs, 8)
    results = []
    for i, names in enumerate(layout):
        piece = jnp.concatenate([parts[name] for name in names], axis=0)
        results.append(second_half(*gather(piece, i == 1)))
    return place(me.reshape(1), results, layout, slab)


def solution(mesh):
    return jax.shard_map(
        on_device,
        mesh=mesh,
        in_specs=(
            P("pair", None, None, "occ"),
            P(),
            P(None, "pair"),
            P(None, "pair", None),
            P("pair", None),
        ),
        out_specs=P("occ", None, "pair"),
        check_vma=False,
    )
```
